32 devices in a mesh: rep: 4 (over y, core), fsdp: 8 (over z, x).
Axes of the slice: x: 2, y: 2, z: 4, core: 2. Of those that a mesh axis runs over, the one named last changes fastest.
Arguments:
- dec_input: bfloat16 [96, 176, 768], P(('rep', 'fsdp')), may hold values from -6 to 6
- enc_output: bfloat16 [96, 512, 768], P(('rep', 'fsdp')), may hold values from -6 to 6
- dec_segments: int32 [96, 176], P(('rep', 'fsdp')), may hold values from 0 to 3, as said below
- enc_segments: int32 [96, 512], P(('rep', 'fsdp')), may hold values from 0 to 3, as said below
- cotangent: bfloat16 [96, 176, 768], P(('rep', 'fsdp')), may hold values from -6 to 6
- norm_self: bfloat16 [768], P('fsdp'), may hold values from 0.5 to 1.5
- q_self: bfloat16 [768, 768], P('fsdp'), may hold values from -0.0546875 to 0.0546875
- k_self: bfloat16 [768, 768], P('fsdp'), may hold values from -0.21875 to 0.21875
- v_self: bfloat16 [768, 768], P('fsdp'), may hold values from -0.21875 to 0.21875
- o_self: bfloat16 [768, 768], P('fsdp'), may hold values from -0.625 to 0.625
- rel_table: bfloat16 [32, 12], P('fsdp'), may hold values from -4 to 4
- norm_cross: bfloat16 [768], P('fsdp'), may hold values from 0.5 to 1.5
- q_cross: bfloat16 [768, 768], P('fsdp'), may hold values from -0.0546875 to 0.0546875
- k_cross: bfloat16 [768, 768], P('fsdp'), may hold values from -0.21875 to 0.21875
- v_cross: bfloat16 [768, 768], P('fsdp'), may hold values from -0.21875 to 0.21875
- o_cross: bfloat16 [768, 768], P('fsdp'), may hold values from -0.625 to 0.625
- norm_ffn: bfloat16 [768], P('fsdp'), may hold values from 0.5 to 1.5
- wi_gate: bfloat16 [768, 2048], P('fsdp'), may hold values from -0.21875 to 0.21875
- wi_up: bfloat16 [768, 2048], P('fsdp'), may hold values from -0.21875 to 0.21875
- wo_ffn: bfloat16 [2048, 768], P('fsdp'), may hold values from -0.125 to 0.125
Outputs:
- dec_output: bfloat16 [96, 176, 768], P(('rep', 'fsdp'))
- input_grad: bfloat16 [96, 176, 768], P(('rep', 'fsdp'))
- enc_grad: bfloat16 [96, 512, 768], P(('rep', 'fsdp'))
- grad_norm_self: float32 [768], P('fsdp')
- grad_q_self: float32 [768, 768], P('fsdp')
- grad_k_self: float32 [768, 768], P('fsdp')
- grad_v_self: float32 [768, 768], P('fsdp')
- grad_o_self: float32 [768, 768], P('fsdp')
- grad_rel_table: float32 [32, 12], P('fsdp')
- grad_norm_cross: float32 [768], P('fsdp')
- grad_q_cross: float32 [768, 768], P('fsdp')
- grad_k_cross: float32 [768, 768], P('fsdp')
- grad_v_cross: float32 [768, 768], P('fsdp')
- grad_o_cross: float32 [768, 768], P('fsdp')
- grad_norm_ffn: float32 [768], P('fsdp')
- grad_wi_gate: float32 [768, 2048], P('fsdp')
- grad_wi_up: float32 [768, 2048], P('fsdp')
- grad_wo_ffn: float32 [2048, 768], P('fsdp')
The draws below stay inside these ranges and needn't reach their ends.
Inputs may be any that keep to these rules, and one draw needn't show every extreme that they name: `dec_segments`: each row holds target documents 1, 2 and 3 in this order, each of 22 positions or more, followed by padding 0 on one position or more; document k of a row's targets belongs to document k of the same row's encoder outputs. `enc_segments`: each row holds encoder documents 1, 2 and 3 in this order, each of 64 positions or more, followed by padding 0 on one position or more.
All inputs are finite; a program needn't handle non-finite values.
Results may differ from the reference program's by a relative error of at most 0.025.
The reference program's roundings to bfloat16 on the way count: a program that leaves them out, or rounds other values in their place, can miss the bound.
Values may be sent and summed in bfloat16 or wider, within the bound.
No kernel may reach another device: no remote copies, remote signals or barrier semaphores. Data moves between devices by JAX's collectives and lax.ppermute only.
A program may use at most 192 MiB of HBM per device.

```python
import math
from functools import partial
import jax
import jax.numpy as jnp
from jax import lax

D = 768
HEADS = 12
HEAD = 64
FF = 2048
BUCKETS = 32
MAXDIST = 128
LD = 176
LE = 512
ROWS_DEV = 3
HD = 768
ROWS = 96


def document_ids(key, row_count, length):
    first_key, second_key, third_key = jax.random.split(key, 3)
    lower_bound = length // 8
    upper_bound = 3 * length // 8
    first_cut = jax.random.randint(first_key, (row_count, 1), lower_bound, upper_bound)
    second_cut = first_cut + jax.random.randint(second_key, (row_count, 1), lower_bound, upper_bound)
    end_cut = length - jax.random.randint(third_key, (row_count, 1), 1, lower_bound)
    positions = jnp.arange(length, dtype=jnp.int32)[None, :]
    ids = 1 + (positions >= first_cut).astype(jnp.int32) + (positions >= second_cut).astype(jnp.int32)
    return jnp.where(positions >= end_cut, 0, ids).astype(jnp.int32)


def draw_dec_segments(key, part):
    return document_ids(jax.random.fold_in(key, 11), ROWS, LD)


def draw_enc_segments(key, part):
    return document_ids(jax.random.fold_in(key, 23), ROWS, LE)


def level_of(rng, shape, cuts, smallest, high):
    factor_of = 1.0
    for position, blocks in cuts:
        heights = jax.random.uniform(jax.random.fold_in(jax.random.fold_in(rng, 6), position), (blocks,), jnp.float32, smallest / len(cuts), high / len(cuts))
        factor_of = factor_of * jnp.repeat(jnp.exp(heights), shape[position] // blocks).reshape((-1,) + (1,) * (len(shape) - 1 - position))
    return factor_of


def scatter_about(rng, extent, spread, most, cuts=(), kind=jnp.bfloat16):
    entries = jax.random.normal(rng, extent, jnp.float32) * spread
    if len(cuts) > 0:
        entries = level_of(rng, extent, cuts, -0.22, 0.18) * entries
    return jnp.clip(entries, min=-most, max=most).astype(kind)


def setup_inputs(seed: int = 0) -> dict:
    splits = jax.random.split(jax.random.key(seed), 21)
    return {
        "dec_input": scatter_about(splits[0], (ROWS, LD, D), 1.0, 6.0, ((0, 32),)),
        "enc_output": scatter_about(splits[1], (ROWS, LE, D), 1.0, 6.0, ((0, 32),)),
        "dec_segments": draw_dec_segments(jax.random.fold_in(splits[20], 71), 0),
        "enc_segments": draw_enc_segments(jax.random.fold_in(splits[20], 71), 0),
        "cotangent": scatter_about(splits[4], (ROWS, LD, D), 1.0, 6.0, ((0, 32),)),
        "norm_self": jnp.clip(1.0 + 0.1 * jax.random.normal(splits[5], (D,), jnp.float32), 0.5, 1.5).astype(jnp.bfloat16),
        "q_self": scatter_about(splits[6], (D, HD), (16 * D) ** -0.5, 0.0546875, ((0, 8),)),
        "k_self": scatter_about(splits[7], (D, HD), D ** -0.5, 0.21875, ((0, 8),)),
        "v_self": scatter_about(splits[8], (D, HD), D ** -0.5, 0.21875, ((0, 8),)),
        "o_self": scatter_about(splits[9], (HD, D), (HD // 8) ** -0.5, 0.625, ((0, 8),)),
        "rel_table": scatter_about(splits[10], (BUCKETS, HEADS), 1.0, 4.0, ((0, 8),)),
        "norm_cross": jnp.clip(1.0 + 0.1 * jax.random.normal(splits[11], (D,), jnp.float32), 0.5, 1.5).astype(jnp.bfloat16),
        "q_cross": scatter_about(splits[12], (D, HD), (16 * D) ** -0.5, 0.0546875, ((0, 8),)),
        "k_cross": scatter_about(splits[13], (D, HD), D ** -0.5, 0.21875, ((0, 8),)),
        "v_cross": scatter_about(splits[14], (D, HD), D ** -0.5, 0.21875, ((0, 8),)),
        "o_cross": scatter_about(splits[15], (HD, D), (HD // 8) ** -0.5, 0.625, ((0, 8),)),
        "norm_ffn": jnp.clip(1.0 + 0.1 * jax.random.normal(splits[16], (D,), jnp.float32), 0.5, 1.5).astype(jnp.bfloat16),
        "wi_gate": scatter_about(splits[17], (D, FF), D ** -0.5, 0.21875, ((0, 8),)),
        "wi_up": scatter_about(splits[18], (D, FF), D ** -0.5, 0.21875, ((0, 8),)),
        "wo_ffn": scatter_about(splits[19], (FF, D), FF ** -0.5, 0.125, ((0, 8),)),
    }


norm_epsilon = 1e-06
masked_score = -1000000000.0
largest_bucket = lax.Precision.HIGHEST

@jax.custom_vjp
def low(v):
    return lax.optimization_barrier(v.astype(jnp.bfloat16)).astype(jnp.float32)

@jax.custom_vjp
def low_back(v):
    return v

def low_keep(v):
    return (low(v), None)

def low_pass(kept, grad):
    return (grad,)

def back_keep(v):
    return (v, None)

def back_low(kept, grad):
    return (low(grad),)
low.defvjp(low_keep, low_pass)
low_back.defvjp(back_keep, back_low)

def both_ways(values):
    return low_back(low(values))

def bucket_of(distance):
    exact_part = BUCKETS // 2
    log_part = BUCKETS - exact_part
    bucket = jnp.minimum(distance, exact_part)
    for degree in range(1, log_part):
        threshold = math.ceil(exact_part * (MAXDIST / exact_part) ** (degree / log_part))
        bucket = bucket + (distance >= threshold).astype(jnp.int32)
    return bucket

def bucket_lookup_table(length):
    positions = jnp.arange(length, dtype=jnp.int32)
    distance = jnp.maximum(positions[:, None] - positions[None, :], 0)
    levels = jnp.arange(BUCKETS, dtype=jnp.int32)
    return (bucket_of(distance)[None] == levels[:, None, None]).astype(jnp.float32)

def rms_scale(values, gain):
    return values * lax.rsqrt(lax.optimization_barrier(jnp.mean(values * values, axis=-1, keepdims=True)) + norm_epsilon) * gain

def project(values, matrix):
    return jnp.einsum('rld,de->rle', values, matrix, precision=largest_bucket)

def attend(query_vectors, key_vectors, value_vectors, relative_position_bias, allowed):
    row_count, query_len = (query_vectors.shape[0], query_vectors.shape[1])
    key_len = key_vectors.shape[1]
    query_heads = query_vectors.reshape(row_count, query_len, HEADS, HEAD)
    key_heads = key_vectors.reshape(row_count, key_len, HEADS, HEAD)
    value_heads = value_vectors.reshape(row_count, key_len, HEADS, HEAD)
    scores = jnp.einsum('rqhd,rkhd->rhqk', query_heads, key_heads, precision=largest_bucket) + relative_position_bias
    scores = low_back(jnp.where(allowed[:, None], scores, masked_score))
    attention_weights = low(jax.nn.softmax(scores, axis=-1))
    context = jnp.einsum('rhqk,rkhd->rqhd', attention_weights, value_heads, precision=largest_bucket)
    return both_ways(context.reshape(row_count, query_len, HEADS * HEAD))

def decoder_group(weight_set, group):
    gain_self, query_self, key_self, value_self, out_self, self_bias_table, gain_cross, query_cross, key_cross, value_cross, out_cross, gain_ffn, gate_matrix, up_matrix, down_matrix = weight_set
    dec_rows, enc_rows, dec_ids, enc_ids = group
    decoder_length = dec_rows.shape[1]
    positions = jnp.arange(decoder_length, dtype=jnp.int32)
    causal = positions[:, None] >= positions[None, :]
    self_allowed = (dec_ids[:, :, None] == dec_ids[:, None, :]) & causal[None]
    cross_allowed = dec_ids[:, :, None] == enc_ids[:, None, :]
    relative_position_bias = jnp.einsum('oul,os->sul', bucket_lookup_table(decoder_length), self_bias_table, precision=largest_bucket)
    normed_self = low(rms_scale(dec_rows, gain_self))
    self_context = attend(both_ways(project(normed_self, query_self)), both_ways(project(normed_self, key_self)), both_ways(project(normed_self, value_self)), relative_position_bias, self_allowed)
    middle = dec_rows + low_back(project(self_context, out_self))
    normed_cross = low(rms_scale(middle, gain_cross))
    cross_context = attend(both_ways(project(normed_cross, query_cross)), both_ways(project(enc_rows, key_cross)), both_ways(project(enc_rows, value_cross)), 0.0, cross_allowed)
    late = middle + low_back(project(cross_context, out_cross))
    normed_ffn = low(rms_scale(late, gain_ffn))
    gate_values = low_back(project(normed_ffn, gate_matrix))
    up_values = low_back(project(normed_ffn, up_matrix))
    hidden = low(jax.nn.gelu(gate_values, approximate=True) * up_values)
    return late + low_back(project(hidden, down_matrix))

def reference(dec_input, enc_output, dec_segments, enc_segments, cotangent, norm_self, q_self, k_self, v_self, o_self, rel_table, norm_cross, q_cross, k_cross, v_cross, o_cross, norm_ffn, wi_gate, wi_up, wo_ffn):
    weight_set = tuple((matrix.astype(jnp.float32) for matrix in (norm_self, q_self, k_self, v_self, o_self, rel_table, norm_cross, q_cross, k_cross, v_cross, o_cross, norm_ffn, wi_gate, wi_up, wo_ffn)))
    groups = dec_input.shape[0] // ROWS_DEV
    dec_float = dec_input.astype(jnp.float32).reshape(groups, ROWS_DEV, LD, D)
    enc_float = enc_output.astype(jnp.float32).reshape(groups, ROWS_DEV, LE, D)
    dec_ids = dec_segments.reshape(groups, ROWS_DEV, LD)
    enc_ids = enc_segments.reshape(groups, ROWS_DEV, LE)

    def whole(weights_in, dec_all, enc_all):
        block = jax.checkpoint(partial(decoder_group, weights_in))
        return lax.map(block, (dec_all, enc_all, dec_ids, enc_ids))
    result, pullback = jax.vjp(whole, weight_set, dec_float, enc_float)
    weight_grads, dec_grad, enc_grad = pullback(cotangent.astype(jnp.float32).reshape(result.shape))
    return (result.reshape(dec_input.shape).astype(jnp.bfloat16), dec_grad.reshape(dec_input.shape).astype(jnp.bfloat16), enc_grad.reshape(enc_output.shape).astype(jnp.bfloat16), weight_grads[0], weight_grads[1], weight_grads[2], weight_grads[3], weight_grads[4], weight_grads[5], weight_grads[6], weight_grads[7], weight_grads[8], weight_grads[9], weight_grads[10], weight_grads[11], weight_grads[12], weight_grads[13], weight_grads[14])
```

```python
import functools
import math

import jax
import jax.numpy as jnp
from jax import lax
from jax.experimental import pallas as pl
from jax.experimental.pallas import tpu as pltpu
from jax.sharding import PartitionSpec as P

HEADS = 12
HEAD = 64
BUCKETS = 32
MAXDIST = 128


norm_epsilon = 1e-06
masked_score = -1000000000.0


def bucket_of(distance):
    exact_part = BUCKETS // 2
    log_part = BUCKETS - exact_part
    bucket = jnp.minimum(distance, exact_part)
    for degree in range(1, log_part):
        threshold = math.ceil(exact_part * (MAXDIST / exact_part) ** (degree / log_part))
        bucket = bucket + (distance >= threshold).astype(jnp.int32)
    return bucket


def bucket_lookup_table(length):
    positions = jnp.arange(length, dtype=jnp.int32)
    distance = jnp.maximum(positions[:, None] - positions[None, :], 0)
    levels = jnp.arange(BUCKETS, dtype=jnp.int32)
    return (bucket_of(distance)[None] == levels[:, None, None]).astype(jnp.bfloat16)


PARTS = 4


def rms_scale(values, gain):
    return (
        values * lax.rsqrt(jnp.mean(values * values, axis=-1, keepdims=True) + norm_epsilon) * gain
    )


def gated(gate_values, up_values):
    return jax.nn.gelu(gate_values, approximate=True) * up_values

def project(values, matrix):
    return jnp.einsum("rld,de->rle", values, matrix, preferred_element_type=jnp.float32)


def weight_grad(values, grads):
    return jnp.einsum("rld,rle->de", values, grads, preferred_element_type=jnp.float32)


def back_project(grads, matrix):
    return jnp.einsum("rle,de->rld", grads, matrix, preferred_element_type=jnp.float32)


def split_heads(values):
    return values.reshape(values.shape[0], values.shape[1], HEADS, HEAD)


def attention_scores(query_vectors, key_vectors, relative_position_bias, allowed):
    scores = (
        jnp.einsum(
            "rqhd,rkhd->rhqk",
            split_heads(query_vectors),
            split_heads(key_vectors),
            preferred_element_type=jnp.float32,
        )
        + relative_position_bias
    )
    return jnp.where(allowed[:, None], scores, masked_score)


def attention_forward(query_vectors, key_vectors, value_vectors, relative_position_bias, allowed):
    scores = attention_scores(query_vectors, key_vectors, relative_position_bias, allowed)
    highest_score = jnp.max(scores, axis=-1, keepdims=True)
    expanded = jnp.exp(scores - highest_score)
    totals = jnp.sum(expanded, axis=-1, keepdims=True)
    attention_weights = (expanded / totals).astype(jnp.bfloat16)
    context = jnp.einsum(
        "rhqk,rkhd->rqhd",
        attention_weights,
        split_heads(value_vectors),
        preferred_element_type=jnp.float32,
    )
    return (
        context.reshape(query_vectors.shape).astype(jnp.bfloat16),
        highest_score + jnp.log(totals),
    )


def attention_backward(
    query_vectors,
    key_vectors,
    value_vectors,
    relative_position_bias,
    allowed,
    log_total,
    context_grad,
):
    scores = attention_scores(query_vectors, key_vectors, relative_position_bias, allowed)
    attention_weights = jnp.exp(scores - log_total)
    grad_heads = split_heads(context_grad)
    weight_grads = jnp.einsum(
        "rqhd,rkhd->rhqk",
        grad_heads,
        split_heads(value_vectors),
        preferred_element_type=jnp.float32,
    )
    row_dot = jnp.sum(attention_weights * weight_grads, axis=-1, keepdims=True)
    score_grads = (attention_weights * (weight_grads - row_dot)).astype(jnp.bfloat16)
    query_grads = jnp.einsum(
        "rhqk,rkhd->rqhd", score_grads, split_heads(key_vectors), preferred_element_type=jnp.float32
    )
    key_grads = jnp.einsum(
        "rhqk,rqhd->rkhd",
        score_grads,
        split_heads(query_vectors),
        preferred_element_type=jnp.float32,
    )
    value_grads = jnp.einsum(
        "rhqk,rqhd->rkhd",
        attention_weights.astype(jnp.bfloat16),
        grad_heads,
        preferred_element_type=jnp.float32,
    )
    return (
        query_grads.reshape(query_vectors.shape).astype(jnp.bfloat16),
        key_grads.reshape(key_vectors.shape).astype(jnp.bfloat16),
        value_grads.reshape(value_vectors.shape).astype(jnp.bfloat16),
        score_grads,
    )


CORE, ROW = [(i, i ^ 1) for i in range(4)], [(i, i ^ 2) for i in range(4)]
ACROSS, NEAR, FAR = (
    [(i, i ^ 1) for i in range(8)],
    [(i, i ^ 2) for i in range(8)],
    [(i, i ^ 4) for i in range(8)],
)


def over_core(values):
    return lax.ppermute(values, "rep", CORE)


def over_row(values):
    return lax.ppermute(values, "rep", ROW)


def over_across(values):
    return lax.ppermute(values, "fsdp", ACROSS)


def over_near(values):
    return lax.ppermute(values, "fsdp", NEAR)


def over_far(values):
    return lax.ppermute(values, "fsdp", FAR)


def pick(values, index, axis):
    return lax.dynamic_index_in_dim(values, index, axis, keepdims=False)


def place_pieces(position, pieces, by_shard):
    low, high = pieces[0].shape[2], pieces[2].shape[2]
    rows, columns = low + high, pieces[0].shape[3]
    shape = (8, PARTS, rows, columns) if by_shard else (PARTS, 8, rows, columns)

    def kernel(position_ref, *refs):
        sources, target, semaphores = refs[:8], refs[8], refs[9]
        part, shard = position_ref[0], position_ref[1]
        copies = []
        for core in range(2):
            for kind in range(4):
                for outer in range(2):
                    for inner in range(4):
                        if kind < 2:
                            row, across = kind, outer
                        else:
                            row, across = outer, kind - 2
                        to_part = part ^ (core + 2 * row)
                        to_shard = shard ^ (across + 4 * (inner & 1) + 2 * (inner >> 1))
                        start, size = (0, low) if kind < 2 else (low, high)
                        index = (to_shard, to_part) if by_shard else (to_part, to_shard)
                        copies.append(
                            pltpu.make_async_copy(
                                sources[core * 4 + kind].at[outer, inner],
                                target.at[index[0], index[1], pl.ds(start, size)],
                                semaphores.at[len(copies)],
                            )
                        )
        for copy in copies:
            copy.start()
        for copy in copies:
            copy.wait()

    return pl.pallas_call(
        kernel,
        out_shape=jax.ShapeDtypeStruct(shape, pieces[0].dtype),
        in_specs=[pl.BlockSpec(memory_space=pltpu.SMEM)]
        + [pl.BlockSpec(memory_space=pl.ANY)] * 8,
        out_specs=pl.BlockSpec(memory_space=pl.ANY),
        scratch_shapes=[pltpu.SemaphoreType.DMA((64,))],
    )(position, *pieces)


def gather_parts(parts, position, by_shard=False):
    held = pick(parts, position[0], 0)[None]
    held = jnp.concatenate([held, over_far(held)], 0)
    held = jnp.concatenate([held, over_near(held)], 0)
    half = held.shape[1] // 2
    first, second = held[:, :half], held[:, half:]
    first = jnp.stack([first, over_across(first)])
    second = jnp.stack([second, over_row(second)])
    pieces = [first, over_row(first), second, over_across(second)]
    pieces = pieces + [over_core(piece) for piece in pieces]
    return place_pieces(position, pieces, by_shard)


def gather_small(values, position):
    held = values[None]
    for bit, move in ((2, over_far), (1, over_near), (0, over_across)):
        other = move(held)
        mine = (position[1] >> bit) & 1
        held = jnp.where(mine == 0, jnp.stack([held, other], 1), jnp.stack([other, held], 1))
        held = held.reshape(-1, *values.shape)
    return held


def add_up(kept, received):
    return (kept.astype(jnp.float32) + received.astype(jnp.float32)).astype(jnp.bfloat16)


def scatter_parts(grads, position):
    part, shard = position[0], position[1]
    core, row = part & 1, part >> 1
    across, near, far = shard & 1, (shard >> 1) & 1, shard >> 2
    rows, columns = grads.shape[2], grads.shape[3]
    half = rows // 2
    grads = grads.astype(jnp.bfloat16).reshape(2, 2, 2, 2, 2, rows, columns)
    sums = add_up(pick(grads, core, 1), over_core(pick(grads, 1 - core, 1)))
    first, second = sums[..., :half, :], sums[..., half:, :]
    from_row, from_across = over_row(pick(first, 1 - row, 0)), over_across(pick(second, 1 - across, 3))
    first, second = add_up(pick(first, row, 0), from_row), add_up(pick(second, across, 3), from_across)
    from_across, from_row = over_across(pick(first, 1 - across, 2)), over_row(pick(second, 1 - row, 0))
    first, second = add_up(pick(first, across, 2), from_across), add_up(pick(second, row, 0), from_row)
    sums = jnp.concatenate([first, second], 2)
    sums = add_up(pick(sums, near, 1), over_near(pick(sums, 1 - near, 1)))
    sums = add_up(pick(sums, far, 0), over_far(pick(sums, 1 - far, 0)))
    other = over_row(sums)
    both = jnp.where(row == 0, jnp.stack([sums, other]), jnp.stack([other, sums]))
    others = over_core(both)
    return jnp.where(core == 0, jnp.stack([both, others], 1), jnp.stack([others, both], 1)).reshape(PARTS, rows, columns).astype(jnp.float32)


def total_small(values):
    for move in (over_core, over_row, over_across, over_near, over_far):
        values = values + move(values)
    return values


def shards(
    fast,
    dec_input,
    enc_output,
    dec_segments,
    enc_segments,
    cotangent,
    norm_self,
    q_self,
    k_self,
    v_self,
    o_self,
    rel_table,
    norm_cross,
    q_cross,
    k_cross,
    v_cross,
    o_cross,
    norm_ffn,
    wi_gate,
    wi_up,
    wo_ffn,
):
    gain_rows = norm_self.shape[0]
    table_rows = rel_table.shape[0]
    width = wi_gate.shape[1] // PARTS
    position = jnp.stack([lax.axis_index("rep"), lax.axis_index("fsdp")]).astype(jnp.int32)
    self_parts = jnp.stack([q_self, k_self, v_self, o_self])
    cross_parts = jnp.stack([q_cross, k_cross, v_cross, o_cross])
    inner_parts = jnp.stack(
        [
            jnp.concatenate(
                [wi_gate[:, i * width : (i + 1) * width], wi_up[:, i * width : (i + 1) * width]], 1
            )
            for i in range(PARTS)
        ]
    )
    small = jnp.concatenate([norm_self, norm_cross, norm_ffn, rel_table.reshape(-1)])
    if fast:
        small_all = gather_small(small, position)
        self_matrices = gather_parts(self_parts, position).reshape(PARTS, -1, self_parts.shape[2])
        cross_matrices = gather_parts(cross_parts, position).reshape(PARTS, -1, cross_parts.shape[2])
        inner = gather_parts(inner_parts, position).reshape(PARTS, -1, 2 * width)
        down_parts = wo_ffn.reshape(PARTS, -1, wo_ffn.shape[1])
        down_matrix = gather_parts(down_parts, position, True).reshape(-1, wo_ffn.shape[1])
    else:
        small_all = lax.all_gather(small, "fsdp", axis=0)
        self_matrices = lax.all_gather(self_parts, "fsdp", axis=1, tiled=True)
        cross_matrices = lax.all_gather(cross_parts, "fsdp", axis=1, tiled=True)
        inner = lax.all_gather(inner_parts, "fsdp", axis=1, tiled=True)
        down_matrix = lax.all_gather(wo_ffn, "fsdp", axis=0, tiled=True)
    gain_self = small_all[:, :gain_rows].reshape(-1)
    gain_cross = small_all[:, gain_rows : 2 * gain_rows].reshape(-1)
    gain_ffn = small_all[:, 2 * gain_rows : 3 * gain_rows].reshape(-1)
    self_bias_table = small_all[:, 3 * gain_rows :].reshape(BUCKETS, HEADS)
    query_self, key_self, value_self, out_self = (self_matrices[i] for i in range(4))
    query_cross, key_cross, value_cross, out_cross = (cross_matrices[i] for i in range(4))

    decoder_length = dec_input.shape[1]
    bucket_indices = bucket_lookup_table(decoder_length)
    positions = jnp.arange(decoder_length, dtype=jnp.int32)
    causal = positions[:, None] >= positions[None, :]
    self_allowed = (dec_segments[:, :, None] == dec_segments[:, None, :]) & causal[None]
    cross_allowed = dec_segments[:, :, None] == enc_segments[:, None, :]
    relative_position_bias = jnp.einsum(
        "oul,os->sul", bucket_indices, self_bias_table, preferred_element_type=jnp.float32
    )
    dec_float = dec_input.astype(jnp.float32)
    normed_self = rms_scale(dec_float, gain_self.astype(jnp.float32)).astype(jnp.bfloat16)
    self_queries = project(normed_self, query_self).astype(jnp.bfloat16)
    self_keys = project(normed_self, key_self).astype(jnp.bfloat16)
    self_values = project(normed_self, value_self).astype(jnp.bfloat16)
    self_context, self_total = attention_forward(
        self_queries, self_keys, self_values, relative_position_bias, self_allowed
    )
    middle = dec_float + project(self_context, out_self)
    normed_cross = rms_scale(middle, gain_cross.astype(jnp.float32)).astype(jnp.bfloat16)
    cross_queries = project(normed_cross, query_cross).astype(jnp.bfloat16)
    cross_keys = project(enc_output, key_cross).astype(jnp.bfloat16)
    cross_values = project(enc_output, value_cross).astype(jnp.bfloat16)
    cross_context, cross_total = attention_forward(
        cross_queries, cross_keys, cross_values, 0.0, cross_allowed
    )
    late = middle + project(cross_context, out_cross)
    normed_ffn = rms_scale(late, gain_ffn.astype(jnp.float32)).astype(jnp.bfloat16)

    inner_values = jnp.einsum(
        "rld,pde->prle", normed_ffn, inner, preferred_element_type=jnp.float32
    )
    gate_values, up_values = inner_values[..., :width], inner_values[..., width:]
    hidden = gated(gate_values, up_values).astype(jnp.bfloat16)
    down_blocks = down_matrix.reshape(PARTS, width, -1)
    dec_output = (
        late
        + jnp.einsum("prle,ped->rld", hidden, down_blocks, preferred_element_type=jnp.float32)
    ).astype(jnp.bfloat16)

    grad_down = jnp.einsum(
        "prle,rld->ped", hidden, cotangent, preferred_element_type=jnp.float32
    )
    hidden_grad = jnp.einsum(
        "rld,ped->prle", cotangent, down_blocks, preferred_element_type=jnp.float32
    )
    gated_out, gated_pull = jax.vjp(gated, gate_values, up_values)
    gate_grad, up_grad = gated_pull(hidden_grad)
    inner_back = jnp.concatenate([gate_grad, up_grad], -1).astype(jnp.bfloat16)
    grad_inner = jnp.einsum(
        "rld,prle->pde", normed_ffn, inner_back, preferred_element_type=jnp.float32
    )
    ffn_in_grad = jnp.einsum("prle,pde->rld", inner_back, inner, preferred_element_type=jnp.float32)
    norm_out, norm_pull = jax.vjp(rms_scale, late, gain_ffn.astype(jnp.float32))
    late_part, grad_gain_ffn = norm_pull(ffn_in_grad)
    late_grad = cotangent.astype(jnp.float32) + late_part

    late_gradb = late_grad.astype(jnp.bfloat16)
    grad_out_cross = weight_grad(cross_context, late_gradb)
    cross_context_grad = back_project(late_gradb, out_cross).astype(jnp.bfloat16)
    cross_q_grad, cross_k_grad, cross_v_grad, cross_ds = attention_backward(
        cross_queries, cross_keys, cross_values, 0.0, cross_allowed, cross_total, cross_context_grad
    )
    grad_query_cross = weight_grad(normed_cross, cross_q_grad)
    grad_key_cross = weight_grad(enc_output, cross_k_grad)
    grad_value_cross = weight_grad(enc_output, cross_v_grad)
    enc_grad = (
        back_project(cross_k_grad, key_cross) + back_project(cross_v_grad, value_cross)
    ).astype(jnp.bfloat16)
    cross_in_grad = back_project(cross_q_grad, query_cross)
    norm_out, norm_pull = jax.vjp(rms_scale, middle, gain_cross.astype(jnp.float32))
    middle_part, grad_gain_cross = norm_pull(cross_in_grad)
    middle_grad = late_grad + middle_part

    middle_gradb = middle_grad.astype(jnp.bfloat16)
    grad_out_self = weight_grad(self_context, middle_gradb)
    self_context_grad = back_project(middle_gradb, out_self).astype(jnp.bfloat16)
    self_q_grad, self_k_grad, self_v_grad, self_score_gradient = attention_backward(
        self_queries,
        self_keys,
        self_values,
        relative_position_bias,
        self_allowed,
        self_total,
        self_context_grad,
    )
    table_gradient = jnp.einsum(
        "cgj,tugj->cu", bucket_indices, self_score_gradient, preferred_element_type=jnp.float32
    )
    grad_query_self = weight_grad(normed_self, self_q_grad)
    grad_key_self = weight_grad(normed_self, self_k_grad)
    grad_value_self = weight_grad(normed_self, self_v_grad)
    self_in_grad = (
        back_project(self_q_grad, query_self)
        + back_project(self_k_grad, key_self)
        + back_project(self_v_grad, value_self)
    )
    norm_out, norm_pull = jax.vjp(rms_scale, dec_float, gain_self.astype(jnp.float32))
    input_part, grad_gain_self = norm_pull(self_in_grad)
    input_grad = (middle_grad + input_part).astype(jnp.bfloat16)

    self_grads = jnp.stack(
        [
            g.astype(jnp.bfloat16)
            for g in (grad_query_self, grad_key_self, grad_value_self, grad_out_self)
        ]
    )
    cross_grads = jnp.stack(
        [
            g.astype(jnp.bfloat16)
            for g in (grad_query_cross, grad_key_cross, grad_value_cross, grad_out_cross)
        ]
    )
    inner_grads = grad_inner.astype(jnp.bfloat16)
    down_grads = grad_down.reshape(-1, grad_down.shape[2]).astype(jnp.bfloat16)
    count = grad_gain_self.shape[0] // gain_rows
    small_grads = jnp.concatenate(
        [
            grad_gain_self.reshape(count, -1),
            grad_gain_cross.reshape(count, -1),
            grad_gain_ffn.reshape(count, -1),
            table_gradient.reshape(count, -1),
        ],
        1,
    )
    if fast:
        split = lambda g: g.reshape(PARTS, 8, -1, g.shape[2])
        down_split = down_grads.reshape(8, PARTS, -1, down_grads.shape[1]).transpose(1, 0, 2, 3)
        down_sum = scatter_parts(down_split, position).reshape(wo_ffn.shape)
        inner_sum = scatter_parts(split(inner_grads), position)
        cross_sum = scatter_parts(split(cross_grads), position)
        self_sum = scatter_parts(split(self_grads), position)
        small_sum = pick(total_small(small_grads), position[1], 0)
    else:
        reduce = lambda g, d: lax.psum(
            lax.psum_scatter(g, "fsdp", scatter_dimension=d, tiled=True), "rep"
        ).astype(jnp.float32)
        down_sum = reduce(down_grads, 0)
        inner_sum = reduce(inner_grads, 1)
        cross_sum = reduce(cross_grads, 1)
        self_sum = reduce(self_grads, 1)
        small_sum = reduce(small_grads.reshape(-1), 0)
    gate_sum = inner_sum[:, :, :width].transpose(1, 0, 2).reshape(wi_gate.shape)
    up_sum = inner_sum[:, :, width:].transpose(1, 0, 2).reshape(wi_up.shape)
    return (
        dec_output,
        input_grad,
        enc_grad,
        small_sum[:gain_rows],
        self_sum[0],
        self_sum[1],
        self_sum[2],
        self_sum[3],
        small_sum[3 * gain_rows :].reshape(table_rows, HEADS),
        small_sum[gain_rows : 2 * gain_rows],
        cross_sum[0],
        cross_sum[1],
        cross_sum[2],
        cross_sum[3],
        small_sum[2 * gain_rows : 3 * gain_rows],
        gate_sum,
        up_sum,
        down_sum,
    )


def solution(mesh):
    placed = (
        P(("rep", "fsdp"), None, None),
        P(("rep", "fsdp"), None, None),
        P(("rep", "fsdp"), None),
        P(("rep", "fsdp"), None),
        P(("rep", "fsdp"), None, None),
        P("fsdp"),
        P("fsdp", None),
        P("fsdp", None),
        P("fsdp", None),
        P("fsdp", None),
        P("fsdp", None),
        P("fsdp"),
        P("fsdp", None),
        P("fsdp", None),
        P("fsdp", None),
        P("fsdp", None),
        P("fsdp"),
        P("fsdp", None),
        P("fsdp", None),
        P("fsdp", None),
    )
    fast = mesh.shape["rep"] == 4 and mesh.shape["fsdp"] == 8
    return jax.shard_map(
        functools.partial(shards, fast),
        mesh=mesh,
        in_specs=placed,
        out_specs=(
            P(("rep", "fsdp"), None, None),
            P(("rep", "fsdp"), None, None),
            P(("rep", "fsdp"), None, None),
            P("fsdp"),
            P("fsdp", None),
            P("fsdp", None),
            P("fsdp", None),
            P("fsdp", None),
            P("fsdp", None),
            P("fsdp"),
            P("fsdp", None),
            P("fsdp", None),
            P("fsdp", None),
            P("fsdp", None),
            P("fsdp"),
            P("fsdp", None),
            P("fsdp", None),
            P("fsdp", None),
        ),
        check_vma=False,
    )
```

```python
import math

import jax
import jax.numpy as jnp
from jax import lax
from jax.experimental import pallas as pl
from jax.experimental.pallas import tpu as pltpu
from jax.sharding import PartitionSpec as P

HEADS = 12
HEAD = 64
BUCKETS = 32
MAXDIST = 128


norm_epsilon = 1e-06
masked_score = -1000000000.0


def bucket_of(distance):
    exact_part = BUCKETS // 2
    log_part = BUCKETS - exact_part
    bucket = jnp.minimum(distance, exact_part)
    for degree in range(1, log_part):
        threshold = math.ceil(exact_part * (MAXDIST / exact_part) ** (degree / log_part))
        bucket = bucket + (distance >= threshold).astype(jnp.int32)
    return bucket


def bucket_lookup_table(length):
    positions = jnp.arange(length, dtype=jnp.int32)
    distance = jnp.maximum(positions[:, None] - positions[None, :], 0)
    levels = jnp.arange(BUCKETS, dtype=jnp.int32)
    return (bucket_of(distance)[None] == levels[:, None, None]).astype(jnp.bfloat16)


PARTS = 4


def rms_scale(values, gain):
    return (
        values * lax.rsqrt(jnp.mean(values * values, axis=-1, keepdims=True) + norm_epsilon) * gain
    )


def gated(gate_values, up_values):
    return jax.nn.gelu(gate_values, approximate=True) * up_values


def project(values, matrix):
    return jnp.einsum("rld,de->rle", values, matrix, preferred_element_type=jnp.float32)


def weight_grad(values, grads):
    return jnp.einsum("rld,rle->de", values, grads, preferred_element_type=jnp.float32)


def back_project(grads, matrix):
    return jnp.einsum("rle,de->rld", grads, matrix, preferred_element_type=jnp.float32)


def split_heads(values):
    return values.reshape(values.shape[0], values.shape[1], HEADS, HEAD)


def attention_scores(query_vectors, key_vectors, relative_position_bias, allowed):
    scores = (
        jnp.einsum(
            "rqhd,rkhd->rhqk",
            split_heads(query_vectors),
            split_heads(key_vectors),
            preferred_element_type=jnp.float32,
        )
        + relative_position_bias
    )
    return jnp.where(allowed[:, None], scores, masked_score)


def attention_forward(query_vectors, key_vectors, value_vectors, relative_position_bias, allowed):
    scores = attention_scores(query_vectors, key_vectors, relative_position_bias, allowed)
    highest_score = jnp.max(scores, axis=-1, keepdims=True)
    expanded = jnp.exp(scores - highest_score)
    totals = jnp.sum(expanded, axis=-1, keepdims=True)
    attention_weights = (expanded / totals).astype(jnp.bfloat16)
    context = jnp.einsum(
        "rhqk,rkhd->rqhd",
        attention_weights,
        split_heads(value_vectors),
        preferred_element_type=jnp.float32,
    )
    return (
        context.reshape(query_vectors.shape).astype(jnp.bfloat16),
        highest_score + jnp.log(totals),
    )


def attention_backward(
    query_vectors,
    key_vectors,
    value_vectors,
    relative_position_bias,
    allowed,
    log_total,
    context_grad,
):
    scores = attention_scores(query_vectors, key_vectors, relative_position_bias, allowed)
    attention_weights = jnp.exp(scores - log_total)
    grad_heads = split_heads(context_grad)
    weight_grads = jnp.einsum(
        "rqhd,rkhd->rhqk",
        grad_heads,
        split_heads(value_vectors),
        preferred_element_type=jnp.float32,
    )
    row_dot = jnp.sum(attention_weights * weight_grads, axis=-1, keepdims=True)
    score_grads = (attention_weights * (weight_grads - row_dot)).astype(jnp.bfloat16)
    query_grads = jnp.einsum(
        "rhqk,rkhd->rqhd", score_grads, split_heads(key_vectors), preferred_element_type=jnp.float32
    )
    key_grads = jnp.einsum(
        "rhqk,rqhd->rkhd",
        score_grads,
        split_heads(query_vectors),
        preferred_element_type=jnp.float32,
    )
    value_grads = jnp.einsum(
        "rhqk,rqhd->rkhd",
        attention_weights.astype(jnp.bfloat16),
        grad_heads,
        preferred_element_type=jnp.float32,
    )
    return (
        query_grads.reshape(query_vectors.shape).astype(jnp.bfloat16),
        key_grads.reshape(key_vectors.shape).astype(jnp.bfloat16),
        value_grads.reshape(value_vectors.shape).astype(jnp.bfloat16),
        score_grads,
    )


def shards(
    dec_input,
    enc_output,
    dec_segments,
    enc_segments,
    cotangent,
    norm_self,
    q_self,
    k_self,
    v_self,
    o_self,
    rel_table,
    norm_cross,
    q_cross,
    k_cross,
    v_cross,
    o_cross,
    norm_ffn,
    wi_gate,
    wi_up,
    wo_ffn,
):
    self_set = (
        lax.all_gather(norm_self, "fsdp", axis=0, tiled=True),
        lax.all_gather(q_self, "fsdp", axis=0, tiled=True),
        lax.all_gather(k_self, "fsdp", axis=0, tiled=True),
        lax.all_gather(v_self, "fsdp", axis=0, tiled=True),
        lax.all_gather(o_self, "fsdp", axis=0, tiled=True),
        lax.all_gather(rel_table, "fsdp", axis=0, tiled=True),
    )
    gain_self, query_self, key_self, value_self, out_self, self_bias_table = self_set
    decoder_length = dec_input.shape[1]
    bucket_indices = bucket_lookup_table(decoder_length)
    positions = jnp.arange(decoder_length, dtype=jnp.int32)
    causal = positions[:, None] >= positions[None, :]
    self_allowed = (dec_segments[:, :, None] == dec_segments[:, None, :]) & causal[None]
    cross_allowed = dec_segments[:, :, None] == enc_segments[:, None, :]
    relative_position_bias = jnp.einsum(
        "oul,os->sul", bucket_indices, self_bias_table, preferred_element_type=jnp.float32
    )
    dec_float = dec_input.astype(jnp.float32)
    normed_self = rms_scale(dec_float, gain_self.astype(jnp.float32)).astype(jnp.bfloat16)
    self_queries = project(normed_self, query_self).astype(jnp.bfloat16)
    self_keys = project(normed_self, key_self).astype(jnp.bfloat16)
    self_values = project(normed_self, value_self).astype(jnp.bfloat16)
    self_context, self_total = attention_forward(
        self_queries, self_keys, self_values, relative_position_bias, self_allowed
    )
    middle = dec_float + project(self_context, out_self)
    cross_set = (
        lax.all_gather(norm_cross, "fsdp", axis=0, tiled=True),
        lax.all_gather(q_cross, "fsdp", axis=0, tiled=True),
        lax.all_gather(k_cross, "fsdp", axis=0, tiled=True),
        lax.all_gather(v_cross, "fsdp", axis=0, tiled=True),
        lax.all_gather(o_cross, "fsdp", axis=0, tiled=True),
    )
    gain_cross, query_cross, key_cross, value_cross, out_cross = cross_set
    normed_cross = rms_scale(middle, gain_cross.astype(jnp.float32)).astype(jnp.bfloat16)
    cross_queries = project(normed_cross, query_cross).astype(jnp.bfloat16)
    cross_keys = project(enc_output, key_cross).astype(jnp.bfloat16)
    cross_values = project(enc_output, value_cross).astype(jnp.bfloat16)
    cross_context, cross_total = attention_forward(
        cross_queries, cross_keys, cross_values, 0.0, cross_allowed
    )
    late = middle + project(cross_context, out_cross)
    ffn_set = (
        lax.all_gather(norm_ffn, "fsdp", axis=0, tiled=True),
        lax.all_gather(wi_gate, "fsdp", axis=0, tiled=True),
        lax.all_gather(wi_up, "fsdp", axis=0, tiled=True),
        lax.all_gather(wo_ffn, "fsdp", axis=0, tiled=True),
    )
    gain_ffn, gate_matrix, up_matrix, down_matrix = ffn_set
    normed_ffn = rms_scale(late, gain_ffn.astype(jnp.float32)).astype(jnp.bfloat16)
    gate_values = project(normed_ffn, gate_matrix)
    up_values = project(normed_ffn, up_matrix)
    hidden = gated(gate_values, up_values).astype(jnp.bfloat16)
    dec_output = (late + project(hidden, down_matrix)).astype(jnp.bfloat16)
    ffn_back = (
        lax.all_gather(norm_ffn, "fsdp", axis=0, tiled=True),
        lax.all_gather(wi_gate, "fsdp", axis=0, tiled=True),
        lax.all_gather(wi_up, "fsdp", axis=0, tiled=True),
        lax.all_gather(wo_ffn, "fsdp", axis=0, tiled=True),
    )
    gain_ffn_b, gate_back, up_back, down_back = ffn_back
    grad_down = weight_grad(hidden, cotangent)
    hidden_grad = back_project(cotangent, down_back)
    gated_out, gated_pull = jax.vjp(gated, gate_values, up_values)
    gate_grad, up_grad = gated_pull(hidden_grad)
    gate_grad = gate_grad.astype(jnp.bfloat16)
    up_grad = up_grad.astype(jnp.bfloat16)
    grad_gate = weight_grad(normed_ffn, gate_grad)
    grad_up = weight_grad(normed_ffn, up_grad)
    ffn_in_grad = back_project(gate_grad, gate_back) + back_project(up_grad, up_back)
    norm_out, norm_pull = jax.vjp(rms_scale, late, gain_ffn_b.astype(jnp.float32))
    late_part, grad_gain_ffn = norm_pull(ffn_in_grad)
    late_grad = cotangent.astype(jnp.float32) + late_part
    ffn_sums = (
        lax.psum_scatter(
            grad_gain_ffn.astype(jnp.bfloat16), "fsdp", scatter_dimension=0, tiled=True
        ).astype(jnp.float32),
        lax.psum_scatter(
            grad_gate.astype(jnp.bfloat16), "fsdp", scatter_dimension=0, tiled=True
        ).astype(jnp.float32),
        lax.psum_scatter(
            grad_up.astype(jnp.bfloat16), "fsdp", scatter_dimension=0, tiled=True
        ).astype(jnp.float32),
        lax.psum_scatter(
            grad_down.astype(jnp.bfloat16), "fsdp", scatter_dimension=0, tiled=True
        ).astype(jnp.float32),
    )
    cross_back = (
        lax.all_gather(norm_cross, "fsdp", axis=0, tiled=True),
        lax.all_gather(q_cross, "fsdp", axis=0, tiled=True),
        lax.all_gather(k_cross, "fsdp", axis=0, tiled=True),
        lax.all_gather(v_cross, "fsdp", axis=0, tiled=True),
        lax.all_gather(o_cross, "fsdp", axis=0, tiled=True),
    )
    gain_cross_b, query_cross_b, key_cross_b, value_cross_b, out_cross_b = cross_back
    late_gradb = late_grad.astype(jnp.bfloat16)
    grad_out_cross = weight_grad(cross_context, late_gradb)
    cross_context_grad = back_project(late_gradb, out_cross_b).astype(jnp.bfloat16)
    cross_q_grad, cross_k_grad, cross_v_grad, cross_ds = attention_backward(
        cross_queries, cross_keys, cross_values, 0.0, cross_allowed, cross_total, cross_context_grad
    )
    grad_query_cross = weight_grad(normed_cross, cross_q_grad)
    grad_key_cross = weight_grad(enc_output, cross_k_grad)
    grad_value_cross = weight_grad(enc_output, cross_v_grad)
    enc_grad = (
        back_project(cross_k_grad, key_cross_b) + back_project(cross_v_grad, value_cross_b)
    ).astype(jnp.bfloat16)
    cross_in_grad = back_project(cross_q_grad, query_cross_b)
    norm_out, norm_pull = jax.vjp(rms_scale, middle, gain_cross_b.astype(jnp.float32))
    middle_part, grad_gain_cross = norm_pull(cross_in_grad)
    middle_grad = late_grad + middle_part
    cross_sums = (
        lax.psum_scatter(
            grad_gain_cross.astype(jnp.bfloat16), "fsdp", scatter_dimension=0, tiled=True
        ).astype(jnp.float32),
        lax.psum_scatter(
            grad_query_cross.astype(jnp.bfloat16), "fsdp", scatter_dimension=0, tiled=True
        ).astype(jnp.float32),
        lax.psum_scatter(
            grad_key_cross.astype(jnp.bfloat16), "fsdp", scatter_dimension=0, tiled=True
        ).astype(jnp.float32),
        lax.psum_scatter(
            grad_value_cross.astype(jnp.bfloat16), "fsdp", scatter_dimension=0, tiled=True
        ).astype(jnp.float32),
        lax.psum_scatter(
            grad_out_cross.astype(jnp.bfloat16), "fsdp", scatter_dimension=0, tiled=True
        ).astype(jnp.float32),
    )
    self_back = (
        lax.all_gather(norm_self, "fsdp", axis=0, tiled=True),
        lax.all_gather(q_self, "fsdp", axis=0, tiled=True),
        lax.all_gather(k_self, "fsdp", axis=0, tiled=True),
        lax.all_gather(v_self, "fsdp", axis=0, tiled=True),
        lax.all_gather(o_self, "fsdp", axis=0, tiled=True),
        lax.all_gather(rel_table, "fsdp", axis=0, tiled=True),
    )
    gain_self_b, query_self_b, key_self_b, value_self_b, out_self_b, table_pullback = self_back
    bias_pullback_fn = jnp.einsum(
        "oul,os->sul", bucket_indices, table_pullback, preferred_element_type=jnp.float32
    )
    middle_gradb = middle_grad.astype(jnp.bfloat16)
    grad_out_self = weight_grad(self_context, middle_gradb)
    self_context_grad = back_project(middle_gradb, out_self_b).astype(jnp.bfloat16)
    self_q_grad, self_k_grad, self_v_grad, self_score_gradient = attention_backward(
        self_queries,
        self_keys,
        self_values,
        bias_pullback_fn,
        self_allowed,
        self_total,
        self_context_grad,
    )
    table_gradient = jnp.einsum(
        "cgj,tugj->cu", bucket_indices, self_score_gradient, preferred_element_type=jnp.float32
    )
    grad_query_self = weight_grad(normed_self, self_q_grad)
    grad_key_self = weight_grad(normed_self, self_k_grad)
    grad_value_self = weight_grad(normed_self, self_v_grad)
    self_in_grad = (
        back_project(self_q_grad, query_self_b)
        + back_project(self_k_grad, key_self_b)
        + back_project(self_v_grad, value_self_b)
    )
    norm_out, norm_pull = jax.vjp(rms_scale, dec_float, gain_self_b.astype(jnp.float32))
    input_part, grad_gain_self = norm_pull(self_in_grad)
    input_grad = (middle_grad + input_part).astype(jnp.bfloat16)
    self_sums = (
        lax.psum_scatter(
            grad_gain_self.astype(jnp.bfloat16), "fsdp", scatter_dimension=0, tiled=True
        ).astype(jnp.float32),
        lax.psum_scatter(
            grad_query_self.astype(jnp.bfloat16), "fsdp", scatter_dimension=0, tiled=True
        ).astype(jnp.float32),
        lax.psum_scatter(
            grad_key_self.astype(jnp.bfloat16), "fsdp", scatter_dimension=0, tiled=True
        ).astype(jnp.float32),
        lax.psum_scatter(
            grad_value_self.astype(jnp.bfloat16), "fsdp", scatter_dimension=0, tiled=True
        ).astype(jnp.float32),
        lax.psum_scatter(
            grad_out_self.astype(jnp.bfloat16), "fsdp", scatter_dimension=0, tiled=True
        ).astype(jnp.float32),
        lax.psum_scatter(
            table_gradient.astype(jnp.bfloat16), "fsdp", scatter_dimension=0, tiled=True
        ).astype(jnp.float32),
    )
    summed = (
        lax.psum(self_sums[0].astype(jnp.bfloat16), "rep").astype(jnp.float32),
        lax.psum(self_sums[1].astype(jnp.bfloat16), "rep").astype(jnp.float32),
        lax.psum(self_sums[2].astype(jnp.bfloat16), "rep").astype(jnp.float32),
        lax.psum(self_sums[3].astype(jnp.bfloat16), "rep").astype(jnp.float32),
        lax.psum(self_sums[4].astype(jnp.bfloat16), "rep").astype(jnp.float32),
        lax.psum(self_sums[5].astype(jnp.bfloat16), "rep").astype(jnp.float32),
        lax.psum(cross_sums[0].astype(jnp.bfloat16), "rep").astype(jnp.float32),
        lax.psum(cross_sums[1].astype(jnp.bfloat16), "rep").astype(jnp.float32),
        lax.psum(cross_sums[2].astype(jnp.bfloat16), "rep").astype(jnp.float32),
        lax.psum(cross_sums[3].astype(jnp.bfloat16), "rep").astype(jnp.float32),
        lax.psum(cross_sums[4].astype(jnp.bfloat16), "rep").astype(jnp.float32),
        lax.psum(ffn_sums[0].astype(jnp.bfloat16), "rep").astype(jnp.float32),
        lax.psum(ffn_sums[1].astype(jnp.bfloat16), "rep").astype(jnp.float32),
        lax.psum(ffn_sums[2].astype(jnp.bfloat16), "rep").astype(jnp.float32),
        lax.psum(ffn_sums[3].astype(jnp.bfloat16), "rep").astype(jnp.float32),
    )
    return (
        dec_output,
        input_grad,
        enc_grad,
        summed[0],
        summed[1],
        summed[2],
        summed[3],
        summed[4],
        summed[5],
        summed[6],
        summed[7],
        summed[8],
        summed[9],
        summed[10],
        summed[11],
        summed[12],
        summed[13],
        summed[14],
    )


CORE, ROW = [(i, i ^ 1) for i in range(4)], [(i, i ^ 2) for i in range(4)]
ACROSS, NEAR, FAR = (
    [(i, i ^ 1) for i in range(8)],
    [(i, i ^ 2) for i in range(8)],
    [(i, i ^ 4) for i in range(8)],
)


def over_core(values):
    return lax.ppermute(values, "rep", CORE)


def over_row(values):
    return lax.ppermute(values, "rep", ROW)


def over_across(values):
    return lax.ppermute(values, "fsdp", ACROSS)


def over_near(values):
    return lax.ppermute(values, "fsdp", NEAR)


def over_far(values):
    return lax.ppermute(values, "fsdp", FAR)


def pick(values, index, axis):
    return lax.dynamic_index_in_dim(values, index, axis, keepdims=False)


def gather_pieces(part):
    held = part[None]
    held = jnp.concatenate([held, over_far(held)], 0)
    held = jnp.concatenate([held, over_near(held)], 0)
    half = held.shape[1] // 2
    first, second = held[:, :half], held[:, half:]
    first = jnp.stack([first, over_across(first)])
    second = jnp.stack([second, over_row(second)])
    pieces = [first, over_row(first), second, over_across(second)]
    return pieces + [over_core(piece) for piece in pieces]


def gather_small(values, position):
    held = values[None]
    for bit, move in ((2, over_far), (1, over_near), (0, over_across)):
        other = move(held)
        mine = (position[1] >> bit) & 1
        held = jnp.where(mine == 0, jnp.stack([held, other], 1), jnp.stack([other, held], 1))
        held = held.reshape(-1, *values.shape)
    return held


def add_up(kept, received):
    return (kept.astype(jnp.float32) + received.astype(jnp.float32)).astype(jnp.bfloat16)


def scatter_parts(grads, position, by_shard=False):
    part, shard = position[0], position[1]
    bit = {"core": part & 1, "row": part >> 1, "across": shard & 1, "near": (shard >> 1) & 1, "far": shard >> 2}
    move = {"core": over_core, "row": over_row, "across": over_across, "near": over_near, "far": over_far}
    axes = ["far", "near", "across", "row", "core"] if by_shard else ["row", "core", "far", "near", "across"]
    rows, columns = grads.shape[2], grads.shape[3]
    half = rows // 2

    def fold(values, names, name):
        axis = names.index(name)
        kept, sent = pick(values, bit[name], axis), pick(values, 1 - bit[name], axis)
        return add_up(kept, move[name](sent)), [n for n in names if n != name]

    sums, axes = fold(grads.reshape(2, 2, 2, 2, 2, rows, columns), axes, "core")
    first, first_axes = fold(sums[..., :half, :], axes, "row")
    second, second_axes = fold(sums[..., half:, :], axes, "across")
    first, axes = fold(first, first_axes, "across")
    second, axes = fold(second, second_axes, "row")
    sums = jnp.concatenate([first, second], 2)
    sums, axes = fold(sums, axes, "near")
    sums, axes = fold(sums, axes, "far")
    other = over_row(sums)
    both = jnp.where(bit["row"] == 0, jnp.stack([sums, other]), jnp.stack([other, sums]))
    others = over_core(both)
    both = jnp.where(bit["core"] == 0, jnp.stack([both, others], 1), jnp.stack([others, both], 1))
    return both.reshape(PARTS, rows, columns).astype(jnp.float32)


def total_small(values):
    for move in (over_core, over_row, over_across, over_near, over_far):
        values = values + move(values)
    return values


BF16, F32 = jnp.bfloat16, jnp.float32
VMEM_LIMIT = 58 * 1024 * 1024
ANYWHERE = pl.BlockSpec(memory_space=pl.ANY)
SCALARS = pl.BlockSpec(memory_space=pltpu.SMEM)
LOCAL = pl.BlockSpec(memory_space=pltpu.VMEM)
PAIR = 2 * HEAD
SPAN = 256


def mul(a, b):
    return lax.dot_general(a, b, (((1,), (0,)), ((), ())), preferred_element_type=F32)


def mul_right_t(a, b):
    return lax.dot_general(a, b, (((1,), (1,)), ((), ())), preferred_element_type=F32)


def mul_left_t(a, b):
    return lax.dot_general(a, b, (((0,), (0,)), ((), ())), preferred_element_type=F32)


def shape_of(*shape, kind=BF16):
    return jax.ShapeDtypeStruct(shape, kind)


def call(kernel, outs, operands, specs, scratch=(), flops=0, moved=0, out_specs=None):
    return pl.pallas_call(
        kernel,
        out_shape=outs,
        in_specs=specs,
        out_specs=out_specs if out_specs is not None else [LOCAL] * len(outs),
        scratch_shapes=list(scratch),
        compiler_params=pltpu.CompilerParams(vmem_limit_bytes=VMEM_LIMIT),
        cost_estimate=pl.CostEstimate(flops=flops, transcendentals=0, bytes_accessed=moved),
    )(*operands)


def relative(core, kind, outer, inner):
    row, across = (kind, outer) if kind < 2 else (outer, kind - 2)
    return core + 2 * row, across + 4 * (inner & 1) + 2 * (inner >> 1)


def start_pieces(position_ref, sources, target_ref, semaphore_of, by_shard):
    half = sources[0].shape[2]
    for core in range(2):
        for kind in range(4):
            for outer in range(2):
                for inner in range(4):
                    part, shard = relative(core, kind, outer, inner)
                    part, shard = position_ref[0] ^ part, position_ref[1] ^ shard
                    place = (shard, part) if by_shard else (part, shard)
                    pltpu.make_async_copy(
                        sources[core * 4 + kind].at[outer, inner],
                        target_ref.at[place[0], place[1], pl.ds((kind // 2) * half, half)],
                        semaphore_of(place[0]),
                    ).start()


def wait_block(target_ref, index, semaphore):
    pltpu.make_async_copy(target_ref.at[index], target_ref.at[index], semaphore).wait()


def matrix(ref, index):
    block = ref[index]
    return block.reshape(-1, block.shape[-1])


def normed(values, gain):
    scale = lax.rsqrt(jnp.mean(values * values, axis=-1, keepdims=True) + norm_epsilon)
    return values * scale * gain


def norm_back(values, gain, grads):
    scale = lax.rsqrt(jnp.mean(values * values, axis=-1, keepdims=True) + norm_epsilon)
    weighted = grads * gain
    mean = jnp.mean(weighted * values, axis=-1, keepdims=True)
    return (
        scale * weighted - values * (scale * scale * scale * mean),
        jnp.sum(grads * values * scale, axis=0, keepdims=True),
    )


def spread_pair(pair):
    low = lax.broadcasted_iota(jnp.int32, pair.shape, 1) < HEAD
    zero = jnp.zeros_like(pair)
    return jnp.concatenate([jnp.where(low, pair, zero), jnp.where(low, zero, pair)], 0)


def join_pair(both):
    rows = both.shape[0] // 2
    low = lax.broadcasted_iota(jnp.int32, (rows, PAIR), 1) < HEAD
    return jnp.where(low, both[:rows], both[rows:])


def twice(values):
    return jnp.concatenate([values, values], 0)


def distance_levels(backward):
    place = lax.broadcasted_iota(jnp.int32, (BUCKETS, SPAN), 1)
    distance = (SPAN - place) % SPAN if backward else place
    level = lax.broadcasted_iota(jnp.int32, (BUCKETS, SPAN), 0)
    return (bucket_of(distance) == level).astype(F32)


def fill_bias(table_ref, bias_ref, length):
    rows = mul_left_t(table_ref[...], distance_levels(True).astype(BF16))
    for head in range(HEADS):
        row = jnp.broadcast_to(rows[head : head + 1], (length, SPAN))
        bias_ref[head] = pltpu.roll(row, 0, 1, stride=1, stride_axis=0)[:, :length]


def self_mask(column_ref, row_ref, row, length):
    near = column_ref[pl.ds(row * length, length), :] == row_ref[pl.ds(row, 1), :]
    i = lax.broadcasted_iota(jnp.int32, (length, length), 0)
    j = lax.broadcasted_iota(jnp.int32, (length, length), 1)
    return near & (j <= i)


def cross_mask(column_ref, row_ref, row, length):
    return column_ref[pl.ds(row * length, length), :] == row_ref[pl.ds(row, 1), :]


def put_totals(totals_ref, row, pair, totals, length):
    lane = lax.broadcasted_iota(jnp.int32, (length, 128), 1)
    rows = pl.ds(row * length, length)
    held = totals_ref[rows, :]
    held = jnp.where(lane == 2 * pair, totals[:length], held)
    totals_ref[rows, :] = jnp.where(lane == 2 * pair + 1, totals[length:], held)


def get_totals(totals_ref, row, pair, length):
    lane = lax.broadcasted_iota(jnp.int32, (length, 128), 1)
    held = totals_ref[pl.ds(row * length, length), :]
    of = lambda head: jnp.sum(jnp.where(lane == head, held, 0.0), axis=1, keepdims=True)
    return jnp.concatenate([of(2 * pair), of(2 * pair + 1)], 0)


def attend_pairs(rows, length, keys_length, mask_of, q_ref, k_ref, v_ref, c_ref, t_ref, bias_ref):
    def step(index, carry):
        row, pair = index // (HEADS // 2), index % (HEADS // 2)
        lanes = pl.ds(pl.multiple_of(pair * PAIR, PAIR), PAIR)
        mine = pl.ds(pl.multiple_of(row * length, 8), length)
        theirs = pl.ds(pl.multiple_of(row * keys_length, 8), keys_length)
        scores = mul_right_t(spread_pair(q_ref[mine, lanes]), k_ref[theirs, lanes])
        if bias_ref is not None:
            scores = scores + jnp.concatenate([bias_ref[2 * pair], bias_ref[2 * pair + 1]], 0)
        scores = jnp.where(twice(mask_of(row)), scores, masked_score)
        highest = jnp.max(scores, axis=1, keepdims=True)
        expanded = jnp.exp(scores - highest)
        totals = jnp.sum(expanded, axis=1, keepdims=True)
        weights = (expanded * (1.0 / totals)).astype(BF16)
        c_ref[mine, lanes] = join_pair(mul(weights, v_ref[theirs, lanes])).astype(BF16)
        put_totals(t_ref, row, pair, highest + jnp.log(totals), length)
        return carry

    lax.fori_loop(0, rows * (HEADS // 2), step, 0)


def attend_pairs_back(
    rows, length, keys_length, mask_of, q_ref, k_ref, v_ref, t_ref, g_ref, dq_ref, dk_ref, dv_ref, bias_ref, sum_ref
):
    def step(index, carry):
        row, pair = index // (HEADS // 2), index % (HEADS // 2)
        lanes = pl.ds(pl.multiple_of(pair * PAIR, PAIR), PAIR)
        mine = pl.ds(pl.multiple_of(row * length, 8), length)
        theirs = pl.ds(pl.multiple_of(row * keys_length, 8), keys_length)
        queries, keys, values = spread_pair(q_ref[mine, lanes]), k_ref[theirs, lanes], v_ref[theirs, lanes]
        grads = spread_pair(g_ref[mine, lanes])
        scores = mul_right_t(queries, keys)
        if bias_ref is not None:
            scores = scores + jnp.concatenate([bias_ref[2 * pair], bias_ref[2 * pair + 1]], 0)
        scores = jnp.where(twice(mask_of(row)), scores, masked_score)
        weights = jnp.exp(scores - get_totals(t_ref, row, pair, length))
        weight_grads = mul_right_t(grads, values)
        row_dot = jnp.sum(weights * weight_grads, axis=1, keepdims=True)
        score_grads = (weights * (weight_grads - row_dot)).astype(BF16)
        dq_ref[mine, lanes] = join_pair(mul(score_grads, keys)).astype(BF16)
        dk_ref[theirs, lanes] = mul_left_t(score_grads, queries).astype(BF16)
        dv_ref[theirs, lanes] = mul_left_t(weights.astype(BF16), grads).astype(BF16)
        if sum_ref is not None:
            for head in range(2):
                part = score_grads[head * length : (head + 1) * length].astype(F32)
                sum_ref[2 * pair + head] = sum_ref[2 * pair + head] + part
        return carry

    lax.fori_loop(0, rows * (HEADS // 2), step, 0)


def self_forward(position, dec, column, row, gain, table, gain_next, pieces):
    tokens, features = dec.shape
    rows = row.shape[0]
    length = tokens // rows

    def kernel(position_ref, dec_ref, column_ref, row_ref, gain_ref, table_ref, next_ref, *refs):
        sources, (n_ref, q_ref, k_ref, v_ref, c_ref, t_ref, mid_ref, nn_ref, m_ref, bias_ref, semaphores) = refs[:8], refs[8:]
        start_pieces(position_ref, sources, m_ref, lambda index: semaphores.at[index], False)
        fill_bias(table_ref, bias_ref, length)
        n_ref[...] = normed(dec_ref[...].astype(F32), gain_ref[...]).astype(BF16)
        for index in range(PARTS):
            wait_block(m_ref, index, semaphores.at[index])
        for out, index in ((q_ref, 0), (k_ref, 1), (v_ref, 2)):
            out[...] = mul(n_ref[...], matrix(m_ref, index)).astype(BF16)
        t_ref[...] = jnp.zeros_like(t_ref)
        mask = lambda r: self_mask(column_ref, row_ref, r, length)
        attend_pairs(rows, length, length, mask, q_ref, k_ref, v_ref, c_ref, t_ref, bias_ref)
        mid_ref[...] = dec_ref[...].astype(F32) + mul(c_ref[...], matrix(m_ref, 3))
        nn_ref[...] = normed(mid_ref[...], next_ref[...]).astype(BF16)

    big = shape_of(tokens, features)
    return call(
        kernel,
        [big, big, big, big, big, shape_of(tokens, 128, kind=F32), shape_of(tokens, features, kind=F32), big, shape_of(PARTS, 8, features // 8, features)],
        (position, dec, column, row, gain, table, gain_next, *pieces),
        [SCALARS] + [LOCAL] * 6 + [ANYWHERE] * 8,
        [pltpu.VMEM((HEADS, length, length), F32), pltpu.SemaphoreType.DMA((PARTS,))],
        flops=30 * tokens * features * features,
        moved=8 * tokens * features * 2 + 16 * features * features,
    )


def cross_forward(position, middle, normed_cross, enc, column, row, gain_next, pieces):
    tokens, features = middle.shape
    rows, keys_length = row.shape
    length = tokens // rows

    def kernel(position_ref, mid_ref, n_ref, enc_ref, column_ref, row_ref, next_ref, *refs):
        sources, (q_ref, k_ref, v_ref, c_ref, t_ref, late_ref, nn_ref, m_ref, semaphores) = refs[:8], refs[8:]
        start_pieces(position_ref, sources, m_ref, lambda index: semaphores.at[index], False)
        for index in range(PARTS):
            wait_block(m_ref, index, semaphores.at[index])
        q_ref[...] = mul(n_ref[...], matrix(m_ref, 0)).astype(BF16)
        for r in range(rows):
            at = pl.ds(r * keys_length, keys_length)
            k_ref[at, :] = mul(enc_ref[at, :], matrix(m_ref, 1)).astype(BF16)
            v_ref[at, :] = mul(enc_ref[at, :], matrix(m_ref, 2)).astype(BF16)
        t_ref[...] = jnp.zeros_like(t_ref)
        mask = lambda r: cross_mask(column_ref, row_ref, r, length)
        attend_pairs(rows, length, keys_length, mask, q_ref, k_ref, v_ref, c_ref, t_ref, None)
        late_ref[...] = mid_ref[...] + mul(c_ref[...], matrix(m_ref, 3))
        nn_ref[...] = normed(late_ref[...], next_ref[...]).astype(BF16)

    big, keys = shape_of(tokens, features), shape_of(enc.shape[0], features)
    return call(
        kernel,
        [big, keys, keys, big, shape_of(tokens, 128, kind=F32), shape_of(tokens, features, kind=F32), big, shape_of(PARTS, 8, features // 8, features)],
        (position, middle, normed_cross, enc, column, row, gain_next, *pieces),
        [SCALARS] + [LOCAL] * 6 + [ANYWHERE] * 8,
        [pltpu.SemaphoreType.DMA((PARTS,))],
        flops=12 * (tokens + enc.shape[0]) * features * features,
        moved=10 * tokens * features * 2 + 16 * features * features + enc.size * 6,
    )


def feed_forward(position, late, normed_ffn, cotangent, gain, inner, down):
    tokens, features = late.shape
    wide = inner[0].shape[3] // 2
    each = wide // 2
    blocks = 8
    inner_shape = (PARTS, 8, features // 8, 2 * wide)
    down_shape = (8, PARTS, each // PARTS, features)

    def kernel(position_ref, late_ref, n_ref, cot_ref, gain_ref, *refs):
        inner_sources, down_sources = refs[:8], refs[8:16]
        out_ref, lg_ref, lgb_ref, gg_ref, di_ref, dd_ref = refs[16:22]
        flat_ref, sum_ref, back_ref, inner_ref, down_ref, inner_done, down_done = refs[22:]
        step = pl.program_id(0)

        @pl.when(step == 0)
        def _():
            start_pieces(position_ref, inner_sources, inner_ref, lambda index: inner_done.at[index], False)
            start_pieces(position_ref, down_sources, down_ref, lambda index: down_done.at[index], True)
            flat_ref[...] = n_ref[...].T
            sum_ref[...] = jnp.zeros_like(sum_ref)
            back_ref[...] = jnp.zeros_like(back_ref)

        @pl.when(step % 2 == 0)
        def _():
            wait_block(inner_ref, step // 2, inner_done.at[step // 2])

        wait_block(down_ref, step, down_done.at[step])
        inner_block = inner_ref[step // 2, :, :, pl.ds(pl.multiple_of((step % 2) * wide, wide), wide)].reshape(features, wide)
        down_block = down_ref[step].reshape(each, features)
        both = mul(n_ref[...], inner_block)
        hidden_grad = mul_right_t(cot_ref[...], down_block)
        gate, up = both[:, :each], both[:, each:]
        inside = math.sqrt(2 / math.pi) * (gate + 0.044715 * (gate * gate * gate))
        bent = jnp.tanh(inside)
        half = 0.5 * (1.0 + bent)
        swish = gate * half
        hidden = (swish * up).astype(BF16)
        slope = half + 0.5 * gate * (1.0 - bent * bent) * (
            math.sqrt(2 / math.pi) * (1.0 + 3 * 0.044715 * (gate * gate))
        )
        grads = jnp.concatenate([hidden_grad * up * slope, hidden_grad * swish], 1).astype(BF16)
        sum_ref[...] += mul(hidden, down_block)
        back_ref[...] += mul_right_t(grads, inner_block)
        di_ref[0] = mul(flat_ref[...], grads).astype(BF16)
        dd_ref[...] = mul_left_t(hidden, cot_ref[...]).astype(BF16)

        @pl.when(step == blocks - 1)
        def _():
            out_ref[...] = (late_ref[...] + sum_ref[...]).astype(BF16)
            part, gain_grad = norm_back(late_ref[...], gain_ref[...], back_ref[...])
            grad = cot_ref[...].astype(F32) + part
            lg_ref[...] = grad
            lgb_ref[...] = grad.astype(BF16)
            gg_ref[...] = gain_grad

    whole = lambda a: pl.BlockSpec(a.shape, lambda i: (0,) * len(a.shape))
    big = shape_of(tokens, features)
    outs = [big, shape_of(tokens, features, kind=F32), big, shape_of(1, features, kind=F32), shape_of(PARTS, features, 2 * wide), shape_of(8 * each, features)]
    inner_spec = pl.BlockSpec((1, features, wide), lambda i: (i // 2, 0, i % 2))
    down_spec = pl.BlockSpec((each, features), lambda i: (i, 0))
    return pl.pallas_call(
        kernel,
        grid=(blocks,),
        out_shape=outs,
        in_specs=[SCALARS, whole(late), whole(normed_ffn), whole(cotangent), whole(gain)] + [ANYWHERE] * 16,
        out_specs=[whole(o) for o in outs[:4]] + [inner_spec, down_spec],
        scratch_shapes=[
            pltpu.VMEM((features, tokens), BF16),
            pltpu.VMEM((tokens, features), F32),
            pltpu.VMEM((tokens, features), F32),
            pltpu.VMEM(inner_shape, BF16),
            pltpu.VMEM(down_shape, BF16),
            pltpu.SemaphoreType.DMA((PARTS,)),
            pltpu.SemaphoreType.DMA((8,)),
        ],
        compiler_params=pltpu.CompilerParams(vmem_limit_bytes=VMEM_LIMIT),
        cost_estimate=pl.CostEstimate(
            flops=18 * tokens * features * 8 * each, transcendentals=0, bytes_accessed=4 * 9437184
        ),
    )(position, late, normed_ffn, cotangent, gain, *inner, *down)


def cross_backward(late_grad, late_gradb, middle, q, k, v, totals, column, row, gain, matrices):
    tokens, features = middle.shape
    rows, keys_length = row.shape
    length = tokens // rows

    def kernel(lg_ref, lgb_ref, mid_ref, q_ref, k_ref, v_ref, t_ref, column_ref, row_ref, gain_ref, m_ref, dq_ref, dk_ref, dv_ref, mg_ref, mgb_ref, gg_ref, g_ref):
        g_ref[...] = mul_right_t(lgb_ref[...], m_ref[3]).astype(BF16)
        mask = lambda r: cross_mask(column_ref, row_ref, r, length)
        attend_pairs_back(rows, length, keys_length, mask, q_ref, k_ref, v_ref, t_ref, g_ref, dq_ref, dk_ref, dv_ref, None, None)
        part, gain_grad = norm_back(mid_ref[...], gain_ref[...], mul_right_t(dq_ref[...], m_ref[0]))
        grad = lg_ref[...] + part
        mg_ref[...] = grad
        mgb_ref[...] = grad.astype(BF16)
        gg_ref[...] = gain_grad

    big, keys = shape_of(tokens, features), shape_of(k.shape[0], features)
    return call(
        kernel,
        [big, keys, keys, shape_of(tokens, features, kind=F32), big, shape_of(1, features, kind=F32)],
        (late_grad, late_gradb, middle, q, k, v, totals, column, row, gain, matrices),
        [LOCAL] * 11,
        [pltpu.VMEM((tokens, features), BF16)],
        flops=4 * tokens * features * features,
        moved=30 * tokens * features * 2,
    )


def self_backward(middle_grad, middle_gradb, dec, q, k, v, totals, column, row, gain, table, matrices):
    tokens, features = dec.shape
    rows = row.shape[0]
    length = tokens // rows

    def kernel(mg_ref, mgb_ref, dec_ref, q_ref, k_ref, v_ref, t_ref, column_ref, row_ref, gain_ref, table_ref, m_ref, dq_ref, dk_ref, dv_ref, ig_ref, gg_ref, tg_ref, g_ref, bias_ref, sum_ref):
        fill_bias(table_ref, bias_ref, length)
        g_ref[...] = mul_right_t(mgb_ref[...], m_ref[3]).astype(BF16)
        sum_ref[...] = jnp.zeros_like(sum_ref)
        mask = lambda r: self_mask(column_ref, row_ref, r, length)
        attend_pairs_back(rows, length, length, mask, q_ref, k_ref, v_ref, t_ref, g_ref, dq_ref, dk_ref, dv_ref, bias_ref, sum_ref)
        back = mul_right_t(dq_ref[...], m_ref[0]) + mul_right_t(dk_ref[...], m_ref[1]) + mul_right_t(dv_ref[...], m_ref[2])
        part, gain_grad = norm_back(dec_ref[...].astype(F32), gain_ref[...], back)
        ig_ref[...] = (mg_ref[...] + part).astype(BF16)
        gg_ref[...] = gain_grad
        sums = []
        i = lax.broadcasted_iota(jnp.int32, (length, length), 0)
        j = lax.broadcasted_iota(jnp.int32, (length, length), 1)
        flip = (i + j == length - 1).astype(F32)
        for head in range(HEADS):
            flipped = lax.dot_general(
                flip, sum_ref[head], (((1,), (0,)), ((), ())),
                precision=lax.Precision.HIGHEST, preferred_element_type=F32,
            )
            square = jnp.concatenate([flipped, jnp.zeros((length, SPAN - length), F32)], 1)
            turned = pltpu.roll(square, SPAN - length + 1, 1, stride=1, stride_axis=0)
            sums.append(jnp.sum(turned, axis=0, keepdims=True))
        sums.append(jnp.zeros((16 - HEADS, SPAN), F32))
        tg_ref[...] = lax.dot_general(
            jnp.concatenate(sums, 0), distance_levels(True), (((1,), (1,)), ((), ())),
            precision=lax.Precision.HIGHEST, preferred_element_type=F32,
        )

    big = shape_of(tokens, features)
    return call(
        kernel,
        [big, big, big, big, shape_of(1, features, kind=F32), shape_of(16, BUCKETS, kind=F32)],
        (middle_grad, middle_gradb, dec, q, k, v, totals, column, row, gain, table, matrices),
        [LOCAL] * 12,
        [pltpu.VMEM((tokens, features), BF16), pltpu.VMEM((HEADS, length, length), F32), pltpu.VMEM((HEADS, length, length), F32)],
        flops=8 * tokens * features * features,
        moved=20 * tokens * features * 2,
    )


def four_grads(lefts, rights):
    features = lefts[0].shape[1]

    def kernel(a0, a1, a2, a3, b0, b1, b2, b3, out_ref):
        for index, (a, b) in enumerate(((a0, b0), (a1, b1), (a2, b2), (a3, b3))):
            out_ref[index] = mul_left_t(a[...], b[...]).astype(BF16)

    tokens = sum(a.shape[0] for a in lefts)
    return call(
        kernel,
        [shape_of(4, features, features)],
        (*lefts, *rights),
        [LOCAL] * 8,
        flops=2 * tokens * features * features,
        moved=4 * tokens * features + 8 * features * features,
    )[0]


def key_value_back(dk, dv, key_matrix, value_matrix):
    tokens, features = dk.shape
    block = 512 if tokens % 512 == 0 else tokens

    def kernel(dk_ref, dv_ref, k_ref, v_ref, out_ref):
        out_ref[...] = (mul_right_t(dk_ref[...], k_ref[...]) + mul_right_t(dv_ref[...], v_ref[...])).astype(BF16)

    spec = pl.BlockSpec((block, features), lambda i: (i, 0))
    whole = pl.BlockSpec(key_matrix.shape, lambda i: (0, 0))
    return pl.pallas_call(
        kernel,
        grid=(tokens // block,),
        out_shape=shape_of(tokens, features),
        in_specs=[spec, spec, whole, whole],
        out_specs=spec,
        compiler_params=pltpu.CompilerParams(vmem_limit_bytes=VMEM_LIMIT),
        cost_estimate=pl.CostEstimate(flops=4 * tokens * features * features, transcendentals=0, bytes_accessed=6 * tokens * features + 4 * features * features),
    )(dk, dv, key_matrix, value_matrix)


def fast_shards(
    dec_input,
    enc_output,
    dec_segments,
    enc_segments,
    cotangent,
    norm_self,
    q_self,
    k_self,
    v_self,
    o_self,
    rel_table,
    norm_cross,
    q_cross,
    k_cross,
    v_cross,
    o_cross,
    norm_ffn,
    wi_gate,
    wi_up,
    wo_ffn,
):
    gain_rows = norm_self.shape[0]
    table_rows = rel_table.shape[0]
    features = dec_input.shape[2]
    blocks = 2
    each = wi_gate.shape[1] // (blocks * PARTS)
    part = lax.axis_index("rep")
    position = jnp.stack([part, lax.axis_index("fsdp")]).astype(jnp.int32)
    choose = lambda *values: lax.select_n(part, *values)
    small = jnp.concatenate([norm_self, norm_cross, norm_ffn, rel_table.reshape(-1)])
    small_all = gather_small(small, position)
    self_pieces = gather_pieces(choose(q_self, k_self, v_self, o_self))
    cross_pieces = gather_pieces(choose(q_cross, k_cross, v_cross, o_cross))
    gate_part = lax.dynamic_slice_in_dim(wi_gate, part * (blocks * each), blocks * each, 1)
    up_part = lax.dynamic_slice_in_dim(wi_up, part * (blocks * each), blocks * each, 1)
    inner_pieces = gather_pieces(
        jnp.concatenate(
            [gate_part[:, :each], up_part[:, :each], gate_part[:, each:], up_part[:, each:]], 1
        )
    )
    down_rows = wo_ffn.shape[0] // PARTS
    down_pieces = gather_pieces(lax.dynamic_slice_in_dim(wo_ffn, part * down_rows, down_rows, 0))
    gain_of = lambda i: small_all[:, i * gain_rows : (i + 1) * gain_rows].reshape(1, -1).astype(F32)
    gain_self, gain_cross, gain_ffn = gain_of(0), gain_of(1), gain_of(2)
    table = small_all[:, 3 * gain_rows :].reshape(BUCKETS, HEADS)

    dec = dec_input.reshape(-1, features)
    enc = enc_output.reshape(-1, features)
    cot = cotangent.reshape(-1, features)
    column = dec_segments.reshape(-1, 1)
    n_self, q, k, v, context, totals, middle, n_cross, self_matrices = self_forward(
        position, dec, column, dec_segments, gain_self, table, gain_cross, self_pieces
    )
    cq, ck, cv, cross_context, cross_totals, late, n_ffn, cross_matrices = cross_forward(
        position, middle, n_cross, enc, column, enc_segments, gain_ffn, cross_pieces
    )
    out, late_grad, late_gradb, grad_gain_ffn, grad_inner, grad_down = feed_forward(
        position, late, n_ffn, cot, gain_ffn, inner_pieces, down_pieces
    )
    self_matrices = self_matrices.reshape(PARTS, features, features)
    cross_matrices = cross_matrices.reshape(PARTS, features, features)
    down_sum = scatter_parts(grad_down.reshape(8, PARTS, -1, features), position, True)
    inner_sum = scatter_parts(grad_inner.reshape(PARTS, 8, -1, grad_inner.shape[2]), position)
    dq, dk, dv, middle_grad, middle_gradb, grad_gain_cross = cross_backward(
        late_grad, late_gradb, middle, cq, ck, cv, cross_totals, column, enc_segments, gain_cross, cross_matrices
    )
    cross_grads = four_grads((n_cross, enc, enc, cross_context), (dq, dk, dv, late_gradb))
    enc_grad = key_value_back(dk, dv, cross_matrices[1], cross_matrices[2])
    cross_sum = scatter_parts(cross_grads.reshape(PARTS, 8, -1, features), position)
    sq, sk, sv, input_grad, grad_gain_self, table_gradient = self_backward(
        middle_grad, middle_gradb, dec, q, k, v, totals, column, dec_segments, gain_self, table, self_matrices
    )
    self_grads = four_grads((n_self, n_self, n_self, context), (sq, sk, sv, middle_gradb))
    self_sum = scatter_parts(self_grads.reshape(PARTS, 8, -1, features), position)
    small_grads = jnp.concatenate(
        [
            grad_gain_self.reshape(8, -1),
            grad_gain_cross.reshape(8, -1),
            grad_gain_ffn.reshape(8, -1),
            table_gradient[:HEADS].T.reshape(8, -1),
        ],
        1,
    )
    small_sum = pick(total_small(small_grads), position[1], 0)
    pieces = lambda first: jnp.concatenate(
        [
            inner_sum[i, :, (2 * j + first) * each : (2 * j + first + 1) * each]
            for i in range(PARTS)
            for j in range(blocks)
        ],
        1,
    )
    return (
        out.reshape(dec_input.shape),
        input_grad.reshape(dec_input.shape),
        enc_grad.reshape(enc_output.shape),
        small_sum[:gain_rows],
        self_sum[0],
        self_sum[1],
        self_sum[2],
        self_sum[3],
        small_sum[3 * gain_rows :].reshape(table_rows, HEADS),
        small_sum[gain_rows : 2 * gain_rows],
        cross_sum[0],
        cross_sum[1],
        cross_sum[2],
        cross_sum[3],
        small_sum[2 * gain_rows : 3 * gain_rows],
        pieces(0),
        pieces(1),
        down_sum.reshape(wo_ffn.shape),
    )


def solution(mesh):
    placed = (
        P(("rep", "fsdp"), None, None),
        P(("rep", "fsdp"), None, None),
        P(("rep", "fsdp"), None),
        P(("rep", "fsdp"), None),
        P(("rep", "fsdp"), None, None),
        P("fsdp"),
        P("fsdp", None),
        P("fsdp", None),
        P("fsdp", None),
        P("fsdp", None),
        P("fsdp", None),
        P("fsdp"),
        P("fsdp", None),
        P("fsdp", None),
        P("fsdp", None),
        P("fsdp", None),
        P("fsdp"),
        P("fsdp", None),
        P("fsdp", None),
        P("fsdp", None),
    )
    fast = mesh.shape["rep"] == 4 and mesh.shape["fsdp"] == 8
    return jax.shard_map(
        fast_shards if fast else shards,
        mesh=mesh,
        in_specs=placed,
        out_specs=(
            P(("rep", "fsdp"), None, None),
            P(("rep", "fsdp"), None, None),
            P(("rep", "fsdp"), None, None),
            P("fsdp"),
            P("fsdp", None),
            P("fsdp", None),
            P("fsdp", None),
            P("fsdp", None),
            P("fsdp", None),
            P("fsdp"),
            P("fsdp", None),
            P("fsdp", None),
            P("fsdp", None),
            P("fsdp", None),
            P("fsdp"),
            P("fsdp", None),
            P("fsdp", None),
            P("fsdp", None),
        ),
        check_vma=False,
    )
```

```python
import math

import jax
import jax.numpy as jnp
from jax import lax
from jax.experimental import pallas as pl
from jax.experimental.pallas import tpu as pltpu
from jax.sharding import PartitionSpec as P

HEADS = 12
HEAD = 64
BUCKETS = 32
MAXDIST = 128


norm_epsilon = 1e-06
masked_score = -1000000000.0


def bucket_of(distance):
    exact_part = BUCKETS // 2
    log_part = BUCKETS - exact_part
    bucket = jnp.minimum(distance, exact_part)
    for degree in range(1, log_part):
        threshold = math.ceil(exact_part * (MAXDIST / exact_part) ** (degree / log_part))
        bucket = bucket + (distance >= threshold).astype(jnp.int32)
    return bucket


def bucket_lookup_table(length):
    positions = jnp.arange(length, dtype=jnp.int32)
    distance = jnp.maximum(positions[:, None] - positions[None, :], 0)
    levels = jnp.arange(BUCKETS, dtype=jnp.int32)
    return (bucket_of(distance)[None] == levels[:, None, None]).astype(jnp.bfloat16)


PARTS = 4


def rms_scale(values, gain):
    return (
        values * lax.rsqrt(jnp.mean(values * values, axis=-1, keepdims=True) + norm_epsilon) * gain
    )


def gated(gate_values, up_values):
    return jax.nn.gelu(gate_values, approximate=True) * up_values


def project(values, matrix):
    return jnp.einsum("rld,de->rle", values, matrix, preferred_element_type=jnp.float32)


def weight_grad(values, grads):
    return jnp.einsum("rld,rle->de", values, grads, preferred_element_type=jnp.float32)


def back_project(grads, matrix):
    return jnp.einsum("rle,de->rld", grads, matrix, preferred_element_type=jnp.float32)


def split_heads(values):
    return values.reshape(values.shape[0], values.shape[1], HEADS, HEAD)


def attention_scores(query_vectors, key_vectors, relative_position_bias, allowed):
    scores = (
        jnp.einsum(
            "rqhd,rkhd->rhqk",
            split_heads(query_vectors),
            split_heads(key_vectors),
            preferred_element_type=jnp.float32,
        )
        + relative_position_bias
    )
    return jnp.where(allowed[:, None], scores, masked_score)


def attention_forward(query_vectors, key_vectors, value_vectors, relative_position_bias, allowed):
    scores = attention_scores(query_vectors, key_vectors, relative_position_bias, allowed)
    highest_score = jnp.max(scores, axis=-1, keepdims=True)
    expanded = jnp.exp(scores - highest_score)
    totals = jnp.sum(expanded, axis=-1, keepdims=True)
    attention_weights = (expanded / totals).astype(jnp.bfloat16)
    context = jnp.einsum(
        "rhqk,rkhd->rqhd",
        attention_weights,
        split_heads(value_vectors),
        preferred_element_type=jnp.float32,
    )
    return (
        context.reshape(query_vectors.shape).astype(jnp.bfloat16),
        highest_score + jnp.log(totals),
    )


def attention_backward(
    query_vectors,
    key_vectors,
    value_vectors,
    relative_position_bias,
    allowed,
    log_total,
    context_grad,
):
    scores = attention_scores(query_vectors, key_vectors, relative_position_bias, allowed)
    attention_weights = jnp.exp(scores - log_total)
    grad_heads = split_heads(context_grad)
    weight_grads = jnp.einsum(
        "rqhd,rkhd->rhqk",
        grad_heads,
        split_heads(value_vectors),
        preferred_element_type=jnp.float32,
    )
    row_dot = jnp.sum(attention_weights * weight_grads, axis=-1, keepdims=True)
    score_grads = (attention_weights * (weight_grads - row_dot)).astype(jnp.bfloat16)
    query_grads = jnp.einsum(
        "rhqk,rkhd->rqhd", score_grads, split_heads(key_vectors), preferred_element_type=jnp.float32
    )
    key_grads = jnp.einsum(
        "rhqk,rqhd->rkhd",
        score_grads,
        split_heads(query_vectors),
        preferred_element_type=jnp.float32,
    )
    value_grads = jnp.einsum(
        "rhqk,rqhd->rkhd",
        attention_weights.astype(jnp.bfloat16),
        grad_heads,
        preferred_element_type=jnp.float32,
    )
    return (
        query_grads.reshape(query_vectors.shape).astype(jnp.bfloat16),
        key_grads.reshape(key_vectors.shape).astype(jnp.bfloat16),
        value_grads.reshape(value_vectors.shape).astype(jnp.bfloat16),
        score_grads,
    )


def shards(
    dec_input,
    enc_output,
    dec_segments,
    enc_segments,
    cotangent,
    norm_self,
    q_self,
    k_self,
    v_self,
    o_self,
    rel_table,
    norm_cross,
    q_cross,
    k_cross,
    v_cross,
    o_cross,
    norm_ffn,
    wi_gate,
    wi_up,
    wo_ffn,
):
    self_set = (
        lax.all_gather(norm_self, "fsdp", axis=0, tiled=True),
        lax.all_gather(q_self, "fsdp", axis=0, tiled=True),
        lax.all_gather(k_self, "fsdp", axis=0, tiled=True),
        lax.all_gather(v_self, "fsdp", axis=0, tiled=True),
        lax.all_gather(o_self, "fsdp", axis=0, tiled=True),
        lax.all_gather(rel_table, "fsdp", axis=0, tiled=True),
    )
    gain_self, query_self, key_self, value_self, out_self, self_bias_table = self_set
    decoder_length = dec_input.shape[1]
    bucket_indices = bucket_lookup_table(decoder_length)
    positions = jnp.arange(decoder_length, dtype=jnp.int32)
    causal = positions[:, None] >= positions[None, :]
    self_allowed = (dec_segments[:, :, None] == dec_segments[:, None, :]) & causal[None]
    cross_allowed = dec_segments[:, :, None] == enc_segments[:, None, :]
    relative_position_bias = jnp.einsum(
        "oul,os->sul", bucket_indices, self_bias_table, preferred_element_type=jnp.float32
    )
    dec_float = dec_input.astype(jnp.float32)
    normed_self = rms_scale(dec_float, gain_self.astype(jnp.float32)).astype(jnp.bfloat16)
    self_queries = project(normed_self, query_self).astype(jnp.bfloat16)
    self_keys = project(normed_self, key_self).astype(jnp.bfloat16)
    self_values = project(normed_self, value_self).astype(jnp.bfloat16)
    self_context, self_total = attention_forward(
        self_queries, self_keys, self_values, relative_position_bias, self_allowed
    )
    middle = dec_float + project(self_context, out_self)
    cross_set = (
        lax.all_gather(norm_cross, "fsdp", axis=0, tiled=True),
        lax.all_gather(q_cross, "fsdp", axis=0, tiled=True),
        lax.all_gather(k_cross, "fsdp", axis=0, tiled=True),
        lax.all_gather(v_cross, "fsdp", axis=0, tiled=True),
        lax.all_gather(o_cross, "fsdp", axis=0, tiled=True),
    )
    gain_cross, query_cross, key_cross, value_cross, out_cross = cross_set
    normed_cross = rms_scale(middle, gain_cross.astype(jnp.float32)).astype(jnp.bfloat16)
    cross_queries = project(normed_cross, query_cross).astype(jnp.bfloat16)
    cross_keys = project(enc_output, key_cross).astype(jnp.bfloat16)
    cross_values = project(enc_output, value_cross).astype(jnp.bfloat16)
    cross_context, cross_total = attention_forward(
        cross_queries, cross_keys, cross_values, 0.0, cross_allowed
    )
    late = middle + project(cross_context, out_cross)
    ffn_set = (
        lax.all_gather(norm_ffn, "fsdp", axis=0, tiled=True),
        lax.all_gather(wi_gate, "fsdp", axis=0, tiled=True),
        lax.all_gather(wi_up, "fsdp", axis=0, tiled=True),
        lax.all_gather(wo_ffn, "fsdp", axis=0, tiled=True),
    )
    gain_ffn, gate_matrix, up_matrix, down_matrix = ffn_set
    normed_ffn = rms_scale(late, gain_ffn.astype(jnp.float32)).astype(jnp.bfloat16)
    gate_values = project(normed_ffn, gate_matrix)
    up_values = project(normed_ffn, up_matrix)
    hidden = gated(gate_values, up_values).astype(jnp.bfloat16)
    dec_output = (late + project(hidden, down_matrix)).astype(jnp.bfloat16)
    ffn_back = (
        lax.all_gather(norm_ffn, "fsdp", axis=0, tiled=True),
        lax.all_gather(wi_gate, "fsdp", axis=0, tiled=True),
        lax.all_gather(wi_up, "fsdp", axis=0, tiled=True),
        lax.all_gather(wo_ffn, "fsdp", axis=0, tiled=True),
    )
    gain_ffn_b, gate_back, up_back, down_back = ffn_back
    grad_down = weight_grad(hidden, cotangent)
    hidden_grad = back_project(cotangent, down_back)
    gated_out, gated_pull = jax.vjp(gated, gate_values, up_values)
    gate_grad, up_grad = gated_pull(hidden_grad)
    gate_grad = gate_grad.astype(jnp.bfloat16)
    up_grad = up_grad.astype(jnp.bfloat16)
    grad_gate = weight_grad(normed_ffn, gate_grad)
    grad_up = weight_grad(normed_ffn, up_grad)
    ffn_in_grad = back_project(gate_grad, gate_back) + back_project(up_grad, up_back)
    norm_out, norm_pull = jax.vjp(rms_scale, late, gain_ffn_b.astype(jnp.float32))
    late_part, grad_gain_ffn = norm_pull(ffn_in_grad)
    late_grad = cotangent.astype(jnp.float32) + late_part
    ffn_sums = (
        lax.psum_scatter(
            grad_gain_ffn.astype(jnp.bfloat16), "fsdp", scatter_dimension=0, tiled=True
        ).astype(jnp.float32),
        lax.psum_scatter(
            grad_gate.astype(jnp.bfloat16), "fsdp", scatter_dimension=0, tiled=True
        ).astype(jnp.float32),
        lax.psum_scatter(
            grad_up.astype(jnp.bfloat16), "fsdp", scatter_dimension=0, tiled=True
        ).astype(jnp.float32),
        lax.psum_scatter(
            grad_down.astype(jnp.bfloat16), "fsdp", scatter_dimension=0, tiled=True
        ).astype(jnp.float32),
    )
    cross_back = (
        lax.all_gather(norm_cross, "fsdp", axis=0, tiled=True),
        lax.all_gather(q_cross, "fsdp", axis=0, tiled=True),
        lax.all_gather(k_cross, "fsdp", axis=0, tiled=True),
        lax.all_gather(v_cross, "fsdp", axis=0, tiled=True),
        lax.all_gather(o_cross, "fsdp", axis=0, tiled=True),
    )
    gain_cross_b, query_cross_b, key_cross_b, value_cross_b, out_cross_b = cross_back
    late_gradb = late_grad.astype(jnp.bfloat16)
    grad_out_cross = weight_grad(cross_context, late_gradb)
    cross_context_grad = back_project(late_gradb, out_cross_b).astype(jnp.bfloat16)
    cross_q_grad, cross_k_grad, cross_v_grad, cross_ds = attention_backward(
        cross_queries, cross_keys, cross_values, 0.0, cross_allowed, cross_total, cross_context_grad
    )
    grad_query_cross = weight_grad(normed_cross, cross_q_grad)
    grad_key_cross = weight_grad(enc_output, cross_k_grad)
    grad_value_cross = weight_grad(enc_output, cross_v_grad)
    enc_grad = (
        back_project(cross_k_grad, key_cross_b) + back_project(cross_v_grad, value_cross_b)
    ).astype(jnp.bfloat16)
    cross_in_grad = back_project(cross_q_grad, query_cross_b)
    norm_out, norm_pull = jax.vjp(rms_scale, middle, gain_cross_b.astype(jnp.float32))
    middle_part, grad_gain_cross = norm_pull(cross_in_grad)
    middle_grad = late_grad + middle_part
    cross_sums = (
        lax.psum_scatter(
            grad_gain_cross.astype(jnp.bfloat16), "fsdp", scatter_dimension=0, tiled=True
        ).astype(jnp.float32),
        lax.psum_scatter(
            grad_query_cross.astype(jnp.bfloat16), "fsdp", scatter_dimension=0, tiled=True
        ).astype(jnp.float32),
        lax.psum_scatter(
            grad_key_cross.astype(jnp.bfloat16), "fsdp", scatter_dimension=0, tiled=True
        ).astype(jnp.float32),
        lax.psum_scatter(
            grad_value_cross.astype(jnp.bfloat16), "fsdp", scatter_dimension=0, tiled=True
        ).astype(jnp.float32),
        lax.psum_scatter(
            grad_out_cross.astype(jnp.bfloat16), "fsdp", scatter_dimension=0, tiled=True
        ).astype(jnp.float32),
    )
    self_back = (
        lax.all_gather(norm_self, "fsdp", axis=0, tiled=True),
        lax.all_gather(q_self, "fsdp", axis=0, tiled=True),
        lax.all_gather(k_self, "fsdp", axis=0, tiled=True),
        lax.all_gather(v_self, "fsdp", axis=0, tiled=True),
        lax.all_gather(o_self, "fsdp", axis=0, tiled=True),
        lax.all_gather(rel_table, "fsdp", axis=0, tiled=True),
    )
    gain_self_b, query_self_b, key_self_b, value_self_b, out_self_b, table_pullback = self_back
    bias_pullback_fn = jnp.einsum(
        "oul,os->sul", bucket_indices, table_pullback, preferred_element_type=jnp.float32
    )
    middle_gradb = middle_grad.astype(jnp.bfloat16)
    grad_out_self = weight_grad(self_context, middle_gradb)
    self_context_grad = back_project(middle_gradb, out_self_b).astype(jnp.bfloat16)
    self_q_grad, self_k_grad, self_v_grad, self_score_gradient = attention_backward(
        self_queries,
        self_keys,
        self_values,
        bias_pullback_fn,
        self_allowed,
        self_total,
        self_context_grad,
    )
    table_gradient = jnp.einsum(
        "cgj,tugj->cu", bucket_indices, self_score_gradient, preferred_element_type=jnp.float32
    )
    grad_query_self = weight_grad(normed_self, self_q_grad)
    grad_key_self = weight_grad(normed_self, self_k_grad)
    grad_value_self = weight_grad(normed_self, self_v_grad)
    self_in_grad = (
        back_project(self_q_grad, query_self_b)
        + back_project(self_k_grad, key_self_b)
        + back_project(self_v_grad, value_self_b)
    )
    norm_out, norm_pull = jax.vjp(rms_scale, dec_float, gain_self_b.astype(jnp.float32))
    input_part, grad_gain_self = norm_pull(self_in_grad)
    input_grad = (middle_grad + input_part).astype(jnp.bfloat16)
    self_sums = (
        lax.psum_scatter(
            grad_gain_self.astype(jnp.bfloat16), "fsdp", scatter_dimension=0, tiled=True
        ).astype(jnp.float32),
        lax.psum_scatter(
            grad_query_self.astype(jnp.bfloat16), "fsdp", scatter_dimension=0, tiled=True
        ).astype(jnp.float32),
        lax.psum_scatter(
            grad_key_self.astype(jnp.bfloat16), "fsdp", scatter_dimension=0, tiled=True
        ).astype(jnp.float32),
        lax.psum_scatter(
            grad_value_self.astype(jnp.bfloat16), "fsdp", scatter_dimension=0, tiled=True
        ).astype(jnp.float32),
        lax.psum_scatter(
            grad_out_self.astype(jnp.bfloat16), "fsdp", scatter_dimension=0, tiled=True
        ).astype(jnp.float32),
        lax.psum_scatter(
            table_gradient.astype(jnp.bfloat16), "fsdp", scatter_dimension=0, tiled=True
        ).astype(jnp.float32),
    )
    summed = (
        lax.psum(self_sums[0].astype(jnp.bfloat16), "rep").astype(jnp.float32),
        lax.psum(self_sums[1].astype(jnp.bfloat16), "rep").astype(jnp.float32),
        lax.psum(self_sums[2].astype(jnp.bfloat16), "rep").astype(jnp.float32),
        lax.psum(self_sums[3].astype(jnp.bfloat16), "rep").astype(jnp.float32),
        lax.psum(self_sums[4].astype(jnp.bfloat16), "rep").astype(jnp.float32),
        lax.psum(self_sums[5].astype(jnp.bfloat16), "rep").astype(jnp.float32),
        lax.psum(cross_sums[0].astype(jnp.bfloat16), "rep").astype(jnp.float32),
        lax.psum(cross_sums[1].astype(jnp.bfloat16), "rep").astype(jnp.float32),
        lax.psum(cross_sums[2].astype(jnp.bfloat16), "rep").astype(jnp.float32),
        lax.psum(cross_sums[3].astype(jnp.bfloat16), "rep").astype(jnp.float32),
        lax.psum(cross_sums[4].astype(jnp.bfloat16), "rep").astype(jnp.float32),
        lax.psum(ffn_sums[0].astype(jnp.bfloat16), "rep").astype(jnp.float32),
        lax.psum(ffn_sums[1].astype(jnp.bfloat16), "rep").astype(jnp.float32),
        lax.psum(ffn_sums[2].astype(jnp.bfloat16), "rep").astype(jnp.float32),
        lax.psum(ffn_sums[3].astype(jnp.bfloat16), "rep").astype(jnp.float32),
    )
    return (
        dec_output,
        input_grad,
        enc_grad,
        summed[0],
        summed[1],
        summed[2],
        summed[3],
        summed[4],
        summed[5],
        summed[6],
        summed[7],
        summed[8],
        summed[9],
        summed[10],
        summed[11],
        summed[12],
        summed[13],
        summed[14],
    )


CORE, ROW = [(i, i ^ 1) for i in range(4)], [(i, i ^ 2) for i in range(4)]
ACROSS, NEAR, FAR = (
    [(i, i ^ 1) for i in range(8)],
    [(i, i ^ 2) for i in range(8)],
    [(i, i ^ 4) for i in range(8)],
)


def over_core(values):
    return lax.ppermute(values, "rep", CORE)


def over_row(values):
    return lax.ppermute(values, "rep", ROW)


def over_across(values):
    return lax.ppermute(values, "fsdp", ACROSS)


def over_near(values):
    return lax.ppermute(values, "fsdp", NEAR)


def over_far(values):
    return lax.ppermute(values, "fsdp", FAR)


def pick(values, index, axis):
    return lax.dynamic_index_in_dim(values, index, axis, keepdims=False)


def after(value, *others):
    return lax.optimization_barrier((value, *others))[0]


def gather_far(part):
    held = part[None]
    return jnp.concatenate([held, over_far(held)], 0)


def gather_near(held):
    return jnp.concatenate([held, over_near(held)], 0)


def gather_one(held):
    half = held.shape[1] // 16 * 8
    first, second = held[:, :half], held[:, half:]
    return jnp.stack([first, over_across(first)]), jnp.stack([second, over_row(second)])


def gather_two(pair):
    return over_row(pair[0]), over_across(pair[1])


def gather_core(pair):
    return over_core(pair[0]), over_core(pair[1])


def in_order(one, two, core_one, core_two):
    return [one[0], two[0], one[1], two[1], core_one[0], core_two[0], core_one[1], core_two[1]]


def add_up(kept, received):
    return (kept.astype(jnp.float32) + received.astype(jnp.float32)).astype(jnp.bfloat16)


class Scatter:
    MOVES = {"core": over_core, "row": over_row, "across": over_across, "near": over_near, "far": over_far}

    def __init__(self, position, keep, send):
        part, shard = position[0], position[1]
        self.bit = {"core": part & 1, "row": part >> 1, "across": shard & 1, "near": (shard >> 1) & 1, "far": shard >> 2}
        self.shape = keep.shape[2:]
        full = (2, 2, 2, 2) + self.shape
        self.keep, self.got = keep.reshape(full), over_core(send.reshape(full))

    def fold(self, values, names, name):
        axis = names.index(name)
        kept, sent = pick(values, self.bit[name], axis), pick(values, 1 - self.bit[name], axis)
        return kept, sent, [n for n in names if n != name]

    def ready_one(self, *gates):
        got = after(self.got, *gates)
        sums = add_up(self.keep, got)
        half = self.shape[0] // 16 * 8
        names = ["row", "far", "near", "across"]
        self.kept_first, self.sent_first, self.first = self.fold(sums[..., :half, :], names, "row")
        self.kept_second, self.sent_second, self.second = self.fold(sums[..., half:, :], names, "across")
        return self.sent_first, self.sent_second

    def move_one(self):
        self.got_first, self.got_second = over_row(self.sent_first), over_across(self.sent_second)

    def ready_two(self, *gates):
        first = add_up(self.kept_first, after(self.got_first, *gates))
        second = add_up(self.kept_second, after(self.got_second, *gates))
        self.kept_first, self.sent_first, self.first = self.fold(first, self.first, "across")
        self.kept_second, self.sent_second, self.second = self.fold(second, self.second, "row")
        return self.sent_first, self.sent_second

    def move_two(self):
        self.got_first, self.got_second = over_across(self.sent_first), over_row(self.sent_second)

    def ready_three(self, *gates):
        first = add_up(self.kept_first, after(self.got_first, *gates))
        second = add_up(self.kept_second, after(self.got_second, *gates))
        sums = jnp.concatenate([first, second], 2)
        self.kept, self.sent, self.names = self.fold(sums, ["far", "near"], "near")
        return (self.sent,)

    def move_three(self):
        self.got = over_near(self.sent)

    def ready_four(self, *gates):
        sums = add_up(self.kept, after(self.got, *gates))
        self.kept, self.sent, self.names = self.fold(sums, self.names, "far")
        return (self.sent,)

    def move_four(self):
        self.got = over_far(self.sent)

    def sent_now(self):
        return (self.sent,)

    def total(self, *gates):
        self.sums = add_up(self.kept, after(self.got, *gates))
        return self.sums

    def move_row(self):
        self.other = over_row(self.sums)

    def finish(self, *gates):
        sums, other = self.sums, after(self.other, *gates)
        both = jnp.where(self.bit["row"] == 0, jnp.stack([sums, other]), jnp.stack([other, sums]))
        others = over_core(both)
        both = jnp.where(self.bit["core"] == 0, jnp.stack([both, others], 1), jnp.stack([others, both], 1))
        return both.reshape((PARTS,) + self.shape)


BF16, F32 = jnp.bfloat16, jnp.float32
VMEM_LIMIT = 58 * 1024 * 1024
ANYWHERE = pl.BlockSpec(memory_space=pltpu.HBM)
SCALARS = pl.BlockSpec(memory_space=pltpu.SMEM)
LOCAL = pl.BlockSpec(memory_space=pltpu.VMEM)
PAIR = 2 * HEAD
SPAN = 256
EXTRA = 8


def mul(a, b):
    return lax.dot_general(a, b, (((1,), (0,)), ((), ())), preferred_element_type=F32)


def mul_right_t(a, b):
    return lax.dot_general(a, b, (((1,), (1,)), ((), ())), preferred_element_type=F32)


def mul_left_t(a, b):
    return lax.dot_general(a, b, (((0,), (0,)), ((), ())), preferred_element_type=F32)


def exact(a, b, dims):
    return lax.dot_general(
        a, b, (dims, ((), ())), precision=lax.Precision.HIGHEST, preferred_element_type=F32
    )


def shape_of(*shape, kind=BF16):
    return jax.ShapeDtypeStruct(shape, kind)


class Inward:
    def __init__(self, source, target, semaphore):
        self.copy, self.target = pltpu.make_async_copy(source, target, semaphore), target
        self.copy.start()
        self.waiting = True

    def __call__(self):
        if self.waiting:
            self.copy.wait()
            self.waiting = False
        return self.target


class Outward:
    def __init__(self, source, target, semaphore):
        self.copy, self.ref = pltpu.make_async_copy(source, target, semaphore), source
        self.sent = False

    def send(self):
        if not self.sent:
            self.copy.start()
            self.sent = True


def cost_of(micros):
    return pl.CostEstimate(flops=int(micros * 1.15e9), transcendentals=0, bytes_accessed=0)


def part_of(operand):
    array, *where = operand if isinstance(operand, tuple) else (operand,)
    if len(where) == 2:
        return array, (pl.ds(*where),), (where[1],) + array.shape[1:]
    if len(where) == 1:
        return array, (where[0],), array.shape[1:]
    return array, (), array.shape


def call(kernel, outs, operands, raw=(), raw_outs=(), scratch=(), micros=1, position=None):
    parts = [part_of(o) for o in operands]
    n_in, n_out = len(parts), len(outs)
    lead = [] if position is None else [position]

    def body(*refs):
        refs = list(refs)
        take = lambda n: [refs.pop(0) for _ in range(n)]
        place = take(len(lead))
        sources, raws, targets, raw_targets = take(n_in), take(len(raw)), take(n_out), take(len(raw_outs))
        buffers, results = take(n_in), take(n_out)
        in_done, out_done = take(1)[0], take(1)[0]
        inward = [
            Inward(source.at[where] if where else source, buffer, in_done.at[i])
            for i, (source, (_, where, _), buffer) in enumerate(zip(sources, parts, buffers))
        ]
        outward = [Outward(r, t, out_done.at[i]) for i, (r, t) in enumerate(zip(results, targets))]
        kernel(inward, outward, place + raws, raw_targets, refs)
        for each in inward:
            each()
        for each in outward:
            each.send()
        for each in outward:
            each.copy.wait()

    return pl.pallas_call(
        body,
        out_shape=list(outs) + list(raw_outs),
        in_specs=[SCALARS] * len(lead) + [ANYWHERE] * (n_in + len(raw)),
        out_specs=[ANYWHERE] * (n_out + len(raw_outs)),
        scratch_shapes=[pltpu.VMEM(shape, array.dtype) for array, _, shape in parts]
        + [pltpu.VMEM(o.shape, o.dtype) for o in outs]
        + [pltpu.SemaphoreType.DMA((max(n_in, 1),)), pltpu.SemaphoreType.DMA((max(n_out, 1),))]
        + list(scratch),
        compiler_params=pltpu.CompilerParams(vmem_limit_bytes=VMEM_LIMIT),
        cost_estimate=cost_of(micros),
    )(*lead, *[array for array, _, _ in parts], *raw)


def relative(core, kind, outer, inner):
    row, across = (kind, outer) if kind < 2 else (outer, kind - 2)
    return core + 2 * row, across + 4 * (inner & 1) + 2 * (inner >> 1)


def start_pieces(position_ref, sources, target_ref, semaphore_of, by_shard):
    total = target_ref.shape[2]
    low = sources[0].shape[2]
    for core in range(2):
        for kind in range(4):
            for outer in range(2):
                for inner in range(4):
                    part, shard = relative(core, kind, outer, inner)
                    part, shard = position_ref[0] ^ part, position_ref[1] ^ shard
                    place = (shard, part) if by_shard else (part, shard)
                    start, size = (0, low) if kind < 2 else (low, total - low)
                    pltpu.make_async_copy(
                        sources[core * 4 + kind].at[outer, inner, pl.ds(0, size)],
                        target_ref.at[place[0], place[1], pl.ds(start, size)],
                        semaphore_of(place[0]),
                    ).start()


def start_extra(position_ref, sources, rows, target_ref, semaphore):
    skip = rows - sources[0].shape[2]
    for kind in (2, 3):
        for inner in range(4):
            shard = position_ref[1] ^ relative(0, kind, 0, inner)[1]
            pltpu.make_async_copy(
                sources[kind].at[0, inner, pl.ds(skip, EXTRA)], target_ref.at[shard], semaphore
            ).start()


def wait_block(target_ref, index, semaphore):
    pltpu.make_async_copy(target_ref.at[index], target_ref.at[index], semaphore).wait()


def flat(ref):
    block = ref[...]
    return block.reshape(-1, block.shape[-1])


def matrix(ref, index):
    block = ref[index]
    return block.reshape(-1, block.shape[-1])


def normed(values, gain):
    scale = lax.rsqrt(jnp.mean(values * values, axis=-1, keepdims=True) + norm_epsilon)
    return values * scale * gain


def norm_back(values, gain, grads):
    scale = lax.rsqrt(jnp.mean(values * values, axis=-1, keepdims=True) + norm_epsilon)
    weighted = grads * gain
    mean = jnp.mean(weighted * values, axis=-1, keepdims=True)
    return (
        scale * weighted - values * (scale * scale * scale * mean),
        jnp.sum(grads * values * scale, axis=0, keepdims=True),
    )


def spread_pair(pair):
    low = lax.broadcasted_iota(jnp.int32, pair.shape, 1) < HEAD
    zero = jnp.zeros_like(pair)
    return jnp.concatenate([jnp.where(low, pair, zero), jnp.where(low, zero, pair)], 0)


def join_pair(both):
    rows = both.shape[0] // 2
    low = lax.broadcasted_iota(jnp.int32, (rows, PAIR), 1) < HEAD
    return jnp.where(low, both[:rows], both[rows:])


def distance_levels(backward):
    place = lax.broadcasted_iota(jnp.int32, (BUCKETS, SPAN), 1)
    distance = (SPAN - place) % SPAN if backward else place
    level = lax.broadcasted_iota(jnp.int32, (BUCKETS, SPAN), 0)
    return (bucket_of(distance) == level).astype(F32)


def fill_bias(table, bias_ref):
    length = bias_ref.shape[1]
    rows = mul_left_t(table.astype(BF16), distance_levels(True).astype(BF16))
    for head in range(HEADS):
        row = jnp.broadcast_to(rows[head : head + 1], (length, SPAN))
        bias_ref[head] = pltpu.roll(row, 0, 1, stride=1, stride_axis=0)[:, :length]


def mask_twice(column_ref, row_ref, row, causal):
    near = column_ref[...] == row_ref[row : row + 1, :]
    if causal:
        i = lax.broadcasted_iota(jnp.int32, near.shape, 0)
        j = lax.broadcasted_iota(jnp.int32, near.shape, 1)
        near = near & (j <= i)
    return near


def pair_scores(queries, keys, pair, near, bias_ref):
    scores = mul_right_t(queries, keys)
    if bias_ref is not None:
        scores = scores + jnp.concatenate([bias_ref[2 * pair], bias_ref[2 * pair + 1]], 0)
    return jnp.where(jnp.concatenate([near, near], 0), scores, masked_score)


def attend_pairs(near_of, q_ref, k_ref, v_ref, c_ref, t_ref, bias_ref):
    length = q_ref.shape[0]
    lane = lax.broadcasted_iota(jnp.int32, (length, 128), 1)
    t_ref[...] = jnp.zeros_like(t_ref)

    def step(pair, carry):
        lanes = pl.ds(pl.multiple_of(pair * PAIR, PAIR), PAIR)
        scores = pair_scores(spread_pair(q_ref[:, lanes]), k_ref[:, lanes], pair, near_of(), bias_ref)
        highest = jnp.max(scores, axis=1, keepdims=True)
        expanded = jnp.exp(scores - highest)
        totals = jnp.sum(expanded, axis=1, keepdims=True)
        weights = (expanded * (1.0 / totals)).astype(BF16)
        c_ref[:, lanes] = join_pair(mul(weights, v_ref[:, lanes])).astype(BF16)
        totals = highest + jnp.log(totals)
        held = jnp.where(lane == 2 * pair, totals[:length], t_ref[...])
        t_ref[...] = jnp.where(lane == 2 * pair + 1, totals[length:], held)
        return carry

    lax.fori_loop(0, HEADS // 2, step, 0)


def attend_pairs_back(near_of, q_ref, k_ref, v_ref, t_ref, g_ref, dq_ref, dk_ref, dv_ref, bias_ref, sum_ref):
    length = q_ref.shape[0]
    lane = lax.broadcasted_iota(jnp.int32, (length, 128), 1)

    def step(pair, carry):
        lanes = pl.ds(pl.multiple_of(pair * PAIR, PAIR), PAIR)
        queries, keys, values = spread_pair(q_ref[:, lanes]), k_ref[:, lanes], v_ref[:, lanes]
        grads = spread_pair(g_ref[:, lanes])
        scores = pair_scores(queries, keys, pair, near_of(), bias_ref)
        held = t_ref[...]
        of = lambda head: jnp.sum(jnp.where(lane == head, held, 0.0), axis=1, keepdims=True)
        weights = jnp.exp(scores - jnp.concatenate([of(2 * pair), of(2 * pair + 1)], 0))
        weight_grads = mul_right_t(grads, values)
        row_dot = jnp.sum(weights * weight_grads, axis=1, keepdims=True)
        score_grads = (weights * (weight_grads - row_dot)).astype(BF16)
        dq_ref[:, lanes] = join_pair(mul(score_grads, keys)).astype(BF16)
        dk_ref[:, lanes] = mul_left_t(score_grads, queries).astype(BF16)
        dv_ref[:, lanes] = mul_left_t(weights.astype(BF16), grads).astype(BF16)
        if sum_ref is not None:
            for head in range(2):
                sum_ref[2 * pair + head] = score_grads[head * length : (head + 1) * length]
        return carry

    lax.fori_loop(0, HEADS // 2, step, 0)


def self_forward(index, position, dec, column, segments, given):
    rows = segments.shape[0]
    length, features = dec.shape[0] // rows, dec.shape[1]
    first = index == 0

    def kernel(inward, outward, raw, raw_outs, scratch):
        if first:
            position_ref, sources = raw[0], raw[1:]
            m_ref, extra_ref, done, extra_done, m_done = scratch
            start_extra(position_ref, sources, m_ref.shape[2], extra_ref, extra_done)
            start_pieces(position_ref, sources, m_ref, lambda i: done.at[i], False)
            dec_in, column_in, row_in = inward
            gain_ref, table_ref, bias_ref = (o.ref for o in outward[8:])
            pltpu.make_async_copy(extra_ref, extra_ref, extra_done).wait()
            total = jnp.zeros((EXTRA, features), F32)
            for shard in range(8):
                held = extra_ref[shard].astype(F32)
                total = total + held
                table_ref[4 * shard : 4 * shard + 4, :] = held[4:8, :128]
            gain_ref[...] = total
            fill_bias(table_ref[...], bias_ref)
            for out in outward[8:]:
                out.send()

            def weights(i):
                wait_block(m_ref, i, done.at[i])
                pltpu.make_async_copy(m_ref.at[i], raw_outs[i], m_done.at[i]).start()
                return matrix(m_ref, i)
        else:
            dec_in, gain_in, q_in, k_in, v_in, column_in, row_in, bias_in, o_in = inward
            weights = lambda i: flat((q_in, k_in, v_in, o_in)[i]())
            gain_ref = gain_in()
        n_out, q_out, k_out, v_out, c_out, t_out, mid_out, nn_out = outward[:8]
        n_out.ref[...] = normed(dec_in()[...].astype(F32), gain_ref[0:1, :]).astype(BF16)
        n_out.send()
        for out, i in ((q_out, 0), (k_out, 1), (v_out, 2)):
            out.ref[...] = mul(n_out.ref[...], weights(i)).astype(BF16)
            out.send()
        column_ref, row_ref = column_in(), row_in()
        if not first:
            bias_ref = bias_in()
        near_of = lambda: mask_twice(column_ref, row_ref, index, True)
        attend_pairs(near_of, q_out.ref, k_out.ref, v_out.ref, c_out.ref, t_out.ref, bias_ref)
        c_out.send()
        t_out.send()
        mid_out.ref[...] = dec_in()[...].astype(F32) + mul(c_out.ref[...], weights(3))
        mid_out.send()
        nn_out.ref[...] = normed(mid_out.ref[...], gain_ref[1:2, :]).astype(BF16)
        if first:
            for i in range(PARTS):
                pltpu.make_async_copy(m_ref.at[i], raw_outs[i], m_done.at[i]).wait()

    big = shape_of(length, features)
    outs = [big, big, big, big, big, shape_of(length, 128, kind=F32), shape_of(length, features, kind=F32), big]
    dec_row, column_row = (dec, index * length, length), (column, index * length, length)
    cost = dict(micros=11 if first else 8)
    if not first:
        q, k, v, o, gains, bias = given
        return call(kernel, outs, (dec_row, gains, q, k, v, column_row, segments, bias, o), **cost)
    block = shape_of(8, features // 8, features)
    more = [shape_of(EXTRA, features, kind=F32), shape_of(BUCKETS, 128, kind=F32), shape_of(HEADS, length, length, kind=F32)]
    return call(
        kernel,
        outs + more,
        (dec_row, column_row, segments),
        given,
        [block] * PARTS,
        [
            pltpu.VMEM((PARTS,) + block.shape, BF16),
            pltpu.VMEM((8, EXTRA, features), BF16),
            pltpu.SemaphoreType.DMA((PARTS,)),
            pltpu.SemaphoreType.DMA(()),
            pltpu.SemaphoreType.DMA((PARTS,)),
        ],
        position=position,
        **cost,
    )


def cross_forward(index, position, middle, normed_cross, enc, column, segments, gains, given):
    rows, keys_length = segments.shape
    length, features = middle.shape
    first = index == 0

    def kernel(inward, outward, raw, raw_outs, scratch):
        if first:
            position_ref, sources = raw[0], raw[1:]
            m_ref, done, m_done = scratch
            start_pieces(position_ref, sources, m_ref, lambda i: done.at[i], False)
            enc_in, n_in, column_in, row_in, mid_in, gain_in = inward

            def weights(i):
                wait_block(m_ref, i, done.at[i])
                pltpu.make_async_copy(m_ref.at[i], raw_outs[i], m_done.at[i]).start()
                return matrix(m_ref, i)
        else:
            n_in, q_in, enc_in, k_in, v_in, column_in, row_in, o_in, mid_in, gain_in = inward
            weights = lambda i: flat((q_in, k_in, v_in, o_in)[i]())
        q_out, k_out, v_out, c_out, t_out, late_out, nn_out = outward
        for out, taken, i in ((q_out, n_in, 0), (k_out, enc_in, 1), (v_out, enc_in, 2)):
            out.ref[...] = mul(taken()[...], weights(i)).astype(BF16)
            out.send()
        column_ref, row_ref = column_in(), row_in()
        near_of = lambda: mask_twice(column_ref, row_ref, index, False)
        attend_pairs(near_of, q_out.ref, k_out.ref, v_out.ref, c_out.ref, t_out.ref, None)
        c_out.send()
        t_out.send()
        late_out.ref[...] = mid_in()[...] + mul(c_out.ref[...], weights(3))
        late_out.send()
        nn_out.ref[...] = normed(late_out.ref[...], gain_in()[2:3, :]).astype(BF16)
        if first:
            for i in range(PARTS):
                pltpu.make_async_copy(m_ref.at[i], raw_outs[i], m_done.at[i]).wait()

    big, keys = shape_of(length, features), shape_of(keys_length, features)
    outs = [big, keys, keys, big, shape_of(length, 128, kind=F32), shape_of(length, features, kind=F32), big]
    enc_row, column_row = (enc, index * keys_length, keys_length), (column, index * length, length)
    cost = dict(micros=13 if first else 10)
    if not first:
        q, k, v, o = given
        return call(kernel, outs, (normed_cross, q, enc_row, k, v, column_row, segments, o, middle, gains), **cost)
    block = shape_of(8, features // 8, features)
    return call(
        kernel,
        outs,
        (enc_row, normed_cross, column_row, segments, middle, gains),
        given,
        [block] * PARTS,
        [pltpu.VMEM((PARTS,) + block.shape, BF16), pltpu.SemaphoreType.DMA((PARTS,)), pltpu.SemaphoreType.DMA((PARTS,))],
        position=position,
        **cost,
    )


def feed_forward(position, late, normed_ffn, cotangent, gains, inner, down):
    rows = len(late)
    length, features = late[0].shape
    tokens = rows * length
    wide = inner[0].shape[3] // 2
    each = wide // 2
    blocks = 8
    high, low = features // 8, each // PARTS
    inner_shape = (PARTS, 8, high, 2 * wide)
    down_shape = (8, PARTS, low, features)
    inner_rows = high * (2 * wide // 128)
    all_rows = inner_rows + low * (features // 128)

    def kernel(position_ref, cot_ref, gain_ref, *refs):
        late_refs, norm_refs, refs = refs[:rows], refs[rows : 2 * rows], refs[2 * rows :]
        inner_sources, down_sources = refs[:8], refs[8:16]
        out_ref, lg_ref, lgb_ref, gg_ref, keep_ref, send_ref = refs[16:22]
        n_ref, flat_ref, sum_ref, back_ref, inner_ref, down_ref, grads_ref, inner_done, down_done, out_done = refs[22:]
        step = pl.program_id(0)
        core = position_ref[0] & 1

        @pl.when(step == 0)
        def _():
            start_pieces(position_ref, inner_sources, inner_ref, lambda i: inner_done.at[i], False)
            start_pieces(position_ref, down_sources, down_ref, lambda i: down_done.at[i], True)
            for row in range(rows):
                n_ref[row * length : (row + 1) * length, :] = norm_refs[row][...]
            flat_ref[...] = n_ref[...].T
            sum_ref[...] = jnp.zeros_like(sum_ref)
            back_ref[...] = jnp.zeros_like(back_ref)

        @pl.when(step % 2 == 0)
        def _():
            wait_block(inner_ref, step // 2, inner_done.at[step // 2])

        wait_block(down_ref, step, down_done.at[step])
        inner_block = inner_ref[step // 2, :, :, pl.ds(pl.multiple_of((step % 2) * wide, wide), wide)].reshape(features, wide)
        down_block = down_ref[step].reshape(each, features)
        both = mul(n_ref[...], inner_block)
        hidden_grad = mul_right_t(cot_ref[...], down_block)
        gate, up = both[:, :each], both[:, each:]
        inside = math.sqrt(2 / math.pi) * (gate + 0.044715 * (gate * gate * gate))
        bent = jnp.tanh(inside)
        half = 0.5 * (1.0 + bent)
        swish = gate * half
        hidden = (swish * up).astype(BF16)
        slope = half + 0.5 * gate * (1.0 - bent * bent) * (
            math.sqrt(2 / math.pi) * (1.0 + 3 * 0.044715 * (gate * gate))
        )
        grads = jnp.concatenate([hidden_grad * up * slope, hidden_grad * swish], 1).astype(BF16)
        sum_ref[...] += mul(hidden, down_block)
        back_ref[...] += mul_right_t(grads, inner_block)
        inner_grads = mul(flat_ref[...], grads).astype(BF16)
        part = step // 2
        slot, row = (part & 1) ^ core, part >> 1
        for shard in range(8):
            for column in range(wide // 128):
                start = pl.multiple_of(((step % 2) * (wide // 128) + column) * high, 16)
                grads_ref[slot, row, shard, pl.ds(start, high), :] = inner_grads[
                    shard * high : (shard + 1) * high, column * 128 : (column + 1) * 128
                ]
        down_grads = mul_left_t(hidden, cot_ref[...]).astype(BF16)
        for part in range(PARTS):
            for column in range(features // 128):
                start = inner_rows + column * low
                grads_ref[(part & 1) ^ core, part >> 1, step, start : start + low, :] = down_grads[
                    part * low : (part + 1) * low, column * 128 : (column + 1) * 128
                ]

        @pl.when(step == blocks - 1)
        def _():
            pltpu.make_async_copy(grads_ref.at[1], send_ref, out_done.at[1]).start()
            pltpu.make_async_copy(grads_ref.at[0], keep_ref, out_done.at[0]).start()
            values = jnp.concatenate([r[...] for r in late_refs], 0)
            out_ref[...] = (values + sum_ref[...]).astype(BF16)
            back, gain_grad = norm_back(values, gain_ref[2:3, :], back_ref[...])
            grad = cot_ref[...].astype(F32) + back
            lg_ref[...] = grad
            lgb_ref[...] = grad.astype(BF16)
            gg_ref[...] = gain_grad
            pltpu.make_async_copy(grads_ref.at[1], send_ref, out_done.at[1]).wait()
            pltpu.make_async_copy(grads_ref.at[0], keep_ref, out_done.at[0]).wait()

    whole = lambda a: pl.BlockSpec(a.shape, lambda i: (0,) * len(a.shape))
    big = shape_of(tokens, features)
    half = shape_of(2, 8, all_rows, 128)
    outs = [big, shape_of(tokens, features, kind=F32), big, shape_of(1, features, kind=F32), half, half]
    return pl.pallas_call(
        kernel,
        grid=(blocks,),
        out_shape=outs,
        in_specs=[SCALARS, whole(cotangent), whole(gains)] + [whole(a) for a in (*late, *normed_ffn)] + [ANYWHERE] * 16,
        out_specs=[whole(o) for o in outs[:4]] + [ANYWHERE] * 2,
        scratch_shapes=[
            pltpu.VMEM((tokens, features), BF16),
            pltpu.VMEM((features, tokens), BF16),
            pltpu.VMEM((tokens, features), F32),
            pltpu.VMEM((tokens, features), F32),
            pltpu.VMEM(inner_shape, BF16),
            pltpu.VMEM(down_shape, BF16),
            pltpu.VMEM((2, 2, 8, all_rows, 128), BF16),
            pltpu.SemaphoreType.DMA((PARTS,)),
            pltpu.SemaphoreType.DMA((8,)),
            pltpu.SemaphoreType.DMA((2,)),
        ],
        compiler_params=pltpu.CompilerParams(vmem_limit_bytes=VMEM_LIMIT),
        cost_estimate=cost_of(31),
    )(position, cotangent, gains, *late, *normed_ffn, *inner, *down)


def cross_backward(index, late_grad, late_gradb, middle, q, k, v, totals, column, segments, gains, query, output):
    rows, keys_length = segments.shape
    length, features = middle.shape

    def kernel(inward, outward, raw, raw_outs, scratch):
        lgb_in, o_in, k_in, q_in, v_in, t_in, column_in, row_in, m_in, mid_in, gain_in, lg_in = inward
        dq_out, dk_out, dv_out, mg_out, mgb_out, gg_out = outward
        (g_ref,) = scratch
        g_ref[...] = mul_right_t(lgb_in()[...], flat(o_in())).astype(BF16)
        column_ref, row_ref = column_in(), row_in()
        near_of = lambda: mask_twice(column_ref, row_ref, index, False)
        attend_pairs_back(near_of, q_in(), k_in(), v_in(), t_in(), g_ref, dq_out.ref, dk_out.ref, dv_out.ref, None, None)
        for out in (dq_out, dk_out, dv_out):
            out.send()
        part, gain_grad = norm_back(mid_in()[...], gain_in()[1:2, :], mul_right_t(dq_out.ref[...], flat(m_in())))
        gg_out.ref[...] = gain_grad
        grad = lg_in()[...] + part
        mg_out.ref[...] = grad
        mgb_out.ref[...] = grad.astype(BF16)

    big, keys = shape_of(length, features), shape_of(keys_length, features)
    row_of = lambda a: (a, index * length, length)
    return call(
        kernel,
        [big, keys, keys, shape_of(length, features, kind=F32), big, shape_of(1, features, kind=F32)],
        (row_of(late_gradb), output, k, q, v, totals, row_of(column), segments, query, middle, gains, row_of(late_grad)),
        scratch=[pltpu.VMEM((length, features), BF16)],
        micros=10,
    )


def self_backward(index, middle_grad, middle_gradb, dec, q, k, v, totals, column, segments, gains, bias, weights):
    rows = segments.shape[0]
    length, features = middle_grad.shape

    def kernel(inward, outward, raw, raw_outs, scratch):
        mgb_in, o_in, q_in, k_in, v_in, t_in, column_in, row_in, bias_in, wq_in, wk_in, wv_in, dec_in, gain_in, mg_in = inward
        dq_out, dk_out, dv_out, ig_out, gg_out, tg_out = outward
        g_ref, sum_ref = scratch
        g_ref[...] = mul_right_t(mgb_in()[...], flat(o_in())).astype(BF16)
        column_ref, row_ref = column_in(), row_in()
        near_of = lambda: mask_twice(column_ref, row_ref, index, True)
        attend_pairs_back(near_of, q_in(), k_in(), v_in(), t_in(), g_ref, dq_out.ref, dk_out.ref, dv_out.ref, bias_in(), sum_ref)
        for out in (dq_out, dk_out, dv_out):
            out.send()
        back = mul_right_t(dq_out.ref[...], flat(wq_in())) + mul_right_t(dk_out.ref[...], flat(wk_in())) + mul_right_t(dv_out.ref[...], flat(wv_in()))
        part, gain_grad = norm_back(dec_in()[...].astype(F32), gain_in()[0:1, :], back)
        ig_out.ref[...] = (mg_in()[...] + part).astype(BF16)
        ig_out.send()
        gg_out.ref[...] = gain_grad
        sums = []
        i = lax.broadcasted_iota(jnp.int32, (length, length), 0)
        j = lax.broadcasted_iota(jnp.int32, (length, length), 1)
        flip = (i + j == length - 1).astype(BF16)
        for head in range(HEADS):
            flipped = mul(flip, sum_ref[head])
            square = jnp.concatenate([flipped, jnp.zeros((length, SPAN - length), F32)], 1)
            turned = pltpu.roll(square, SPAN - length + 1, 1, stride=1, stride_axis=0)
            sums.append(jnp.sum(turned, axis=0, keepdims=True))
        sums.append(jnp.zeros((128 - HEADS, SPAN), F32))
        tg_out.ref[...] = exact(distance_levels(True), jnp.concatenate(sums, 0), ((1,), (1,)))

    big = shape_of(length, features)
    row_of = lambda a: (a, index * length, length)
    return call(
        kernel,
        [big, big, big, big, shape_of(1, features, kind=F32), shape_of(BUCKETS, 128, kind=F32)],
        (middle_gradb, weights[3], q, k, v, totals, row_of(column), segments, bias, *weights[:3], row_of(dec), gains, middle_grad),
        scratch=[pltpu.VMEM((length, features), BF16), pltpu.VMEM((HEADS, length, length), BF16)],
        micros=11,
    )


def weight_grads(position, lefts, rights, extra=None):
    features = rights[0][0].shape[1] if not isinstance(rights[0][0], tuple) else rights[0][0][0].shape[1]
    high = features // 8
    all_rows = high + (EXTRA if extra else 0)
    known, operands = {}, []

    def place_of(a):
        key = (id(a[0]), a[1]) if isinstance(a, tuple) else (id(a), -1)
        if key not in known:
            known[key] = len(operands)
            operands.append(a)
        return known[key]

    places = [([place_of(a) for a in left], [place_of(b) for b in right]) for left, right in zip(lefts, rights)]
    more = [[place_of(a) for a in group] for group in extra] if extra else []

    def kernel(inward, outward, raw, raw_outs, scratch):
        (position_ref,) = raw
        keep_ref, send_ref = raw_outs
        grads_ref, done = scratch
        core = position_ref[0] & 1
        copies = [
            pltpu.make_async_copy(grads_ref.at[slot, row], (keep_ref, send_ref)[slot].at[row], done.at[2 * slot + row])
            for slot in range(2)
            for row in range(2)
        ]
        if extra:
            groups = []
            for group in more:
                total = inward[group[0]]()[...]
                for i in group[1:]:
                    total = total + inward[i]()[...]
                groups.append(total)
            line = lax.broadcasted_iota(jnp.int32, (EXTRA, features), 0)
            base = jnp.zeros((EXTRA, features), F32)
            for i in range(3):
                base = jnp.where(line == i, groups[i], base)
            row = lax.broadcasted_iota(jnp.int32, (EXTRA, BUCKETS), 0)
            level = lax.broadcasted_iota(jnp.int32, (EXTRA, BUCKETS), 1)
            for shard in range(8):
                chosen = ((row >= 4) & (level == row - 4 + 4 * shard)).astype(F32)
                table = exact(chosen, groups[3], ((1,), (0,)))
                block = base + jnp.concatenate([table, jnp.zeros((EXTRA, features - 128), F32)], 1)
                for slot in range(2):
                    for part in range(2):
                        grads_ref[slot, part, shard, high:, :] = block.astype(BF16)
        for m, (left, right) in enumerate(places):
            total = mul_left_t(inward[left[0]]()[...], inward[right[0]]()[...])
            for i, j in zip(left[1:], right[1:]):
                total = total + mul_left_t(inward[i]()[...], inward[j]()[...])
            total = total.astype(BF16)
            for shard in range(8):
                grads_ref[(m & 1) ^ core, m >> 1, shard, :high, :] = total[shard * high : (shard + 1) * high]
            if m == 1:
                copies[0].start()
                copies[2].start()
        copies[3].start()
        copies[1].start()
        for copy in copies:
            copy.wait()

    half = shape_of(2, 8, all_rows, features)
    return call(
        kernel,
        [],
        operands,
        raw_outs=[half, half],
        scratch=[pltpu.VMEM((2, 2, 8, all_rows, features), BF16), pltpu.SemaphoreType.DMA((4,))],
        micros=13,
        position=position,
    )


def key_value_back(dk, dv, key, value):
    rows = len(dk)
    length, features = dk[0].shape

    def kernel(inward, outward, raw, raw_outs, scratch):
        result_ref, done = scratch
        copies = [pltpu.make_async_copy(result_ref.at[r], raw_outs[0].at[r], done.at[r]) for r in range(rows)]
        for row in range(rows):
            k_in, v_in = (inward[0], inward[2]) if row == 0 else (inward[2 + 2 * row], inward[3 + 2 * row])
            result_ref[row] = (
                mul_right_t(k_in()[...], flat(inward[1]())) + mul_right_t(v_in()[...], flat(inward[3]()))
            ).astype(BF16)
            copies[row].start()
        for copy in copies:
            copy.wait()

    operands = [dk[0], key, dv[0], value]
    for row in range(1, rows):
        operands += [dk[row], dv[row]]
    whole = shape_of(rows, length, features)
    return call(
        kernel,
        [],
        operands,
        raw_outs=[whole],
        scratch=[pltpu.VMEM(whole.shape, BF16), pltpu.SemaphoreType.DMA((rows,))],
        micros=8,
    )[0]


def fast_shards(
    dec_input,
    enc_output,
    dec_segments,
    enc_segments,
    cotangent,
    norm_self,
    q_self,
    k_self,
    v_self,
    o_self,
    rel_table,
    norm_cross,
    q_cross,
    k_cross,
    v_cross,
    o_cross,
    norm_ffn,
    wi_gate,
    wi_up,
    wo_ffn,
):
    rows = dec_input.shape[0]
    gain_rows = norm_self.shape[0]
    table_rows = rel_table.shape[0]
    features = dec_input.shape[2]
    blocks = 2
    each = wi_gate.shape[1] // (blocks * PARTS)
    part, shard = lax.axis_index("rep"), lax.axis_index("fsdp")
    position = jnp.stack([part, shard]).astype(jnp.int32)
    choose = lambda *values: lax.select_n(part, *values)

    extra = jnp.zeros((EXTRA, features), BF16)
    gains_here = jnp.stack([norm_self, norm_cross, norm_ffn])
    extra = lax.dynamic_update_slice(extra, gains_here, (0, shard * gain_rows))
    extra = lax.dynamic_update_slice(extra, rel_table, (4, 0))
    self_part = jnp.concatenate([choose(q_self, k_self, v_self, o_self), extra], 0)
    cross_part = choose(q_cross, k_cross, v_cross, o_cross)
    gate_part = lax.dynamic_slice_in_dim(wi_gate, part * (blocks * each), blocks * each, 1)
    up_part = lax.dynamic_slice_in_dim(wi_up, part * (blocks * each), blocks * each, 1)
    inner_part = jnp.concatenate(
        [gate_part[:, :each], up_part[:, :each], gate_part[:, each:], up_part[:, each:]], 1
    )
    down_rows = wo_ffn.shape[0] // PARTS
    down_part = lax.dynamic_slice_in_dim(wo_ffn, part * down_rows, down_rows, 0)

    s0 = gather_far(self_part)
    c0 = gather_far(after(cross_part, s0))
    s1 = gather_near(s0)
    i0 = gather_far(after(inner_part, c0, s1))
    c1 = gather_near(after(c0, s1))
    s2 = gather_one(s1)
    s3 = gather_two(s2)
    c1 = after(c1, *s2)
    d0 = gather_far(after(down_part, i0, *s2))
    i1 = gather_near(after(i0, *s2))
    s4 = gather_core(s2)
    c2 = gather_one(after(c1, *s3))
    s5 = gather_core(s3)
    self_pieces = in_order(s2, s3, s4, s5)

    dec = dec_input.reshape(-1, features)
    enc = enc_output.reshape(-1, features)
    cot = cotangent.reshape(-1, features)
    column = dec_segments.reshape(-1, 1)

    made = self_forward(0, position, after(dec, c1), column, dec_segments, self_pieces)
    selfs = [made[:8]]
    gains, table, bias, *self_matrices = made[8:]
    given = (*self_matrices, gains, bias)
    c2 = tuple(after(c, made[0]) for c in c2)
    c3 = gather_two(c2)
    i1 = after(i1, made[0])
    d1 = gather_near(after(d0, made[0]))
    c4 = gather_core(c2)
    i2 = gather_one(i1)
    selfs.append(self_forward(1, position, after(dec, *c2, i1), column, dec_segments, given))
    d1 = after(d1, selfs[1][0])
    selfs.append(self_forward(2, position, after(dec, selfs[1][0]), column, dec_segments, given))
    c3 = tuple(after(c, selfs[2][0]) for c in c3)
    i2 = tuple(after(i, selfs[2][0]) for i in i2)
    c5 = gather_core(c3)
    i3 = gather_two(i2)
    given = in_order(c2, c3, c4, c5)
    crosses = []
    cross = lambda row, n, *given: cross_forward(row, position, selfs[row][6], n, enc, column, enc_segments, gains, given)
    made = cross(0, after(selfs[0][7], *i2, d1), *given)
    cross_matrices = made[7:]
    crosses = [made[:7]]
    d1 = after(d1, made[0])
    d2 = gather_one(d1)
    i4 = gather_core(i2)
    crosses.append(cross(1, after(selfs[1][7], d1), *cross_matrices))
    d2 = tuple(after(d, crosses[1][0]) for d in d2)
    d3 = gather_two(d2)
    i3 = tuple(after(i, crosses[1][0]) for i in i3)
    i5 = gather_core(i3)
    d4 = gather_core(d2)
    crosses.append(cross(2, after(selfs[2][7], *i3, *d2), *cross_matrices))
    d3 = tuple(after(d, crosses[2][0]) for d in d3)
    d5 = gather_core(d3)
    out, late_grad, late_gradb, grad_gain_ffn, keep, send = feed_forward(
        position,
        [c[5] for c in crosses],
        [c[6] for c in crosses],
        cot,
        gains,
        in_order(i2, i3, i4, i5),
        in_order(d2, d3, d4, d5),
    )

    ffn_sums = Scatter(position, keep, send)

    def cross_back(row, *gates):
        q, k, v, context, totals, late, n_ffn = crosses[row]
        return cross_backward(
            row, after(late_grad, *gates), late_gradb, selfs[row][6], q, k, v, totals, column, enc_segments, gains, cross_matrices[0], cross_matrices[3]
        )

    def self_back(row, made, *gates):
        n, q, k, v, context, totals, middle, n_cross = selfs[row]
        return self_backward(
            row, after(made[3], *gates), made[4], dec, q, k, v, totals, column, dec_segments, gains, bias, self_matrices
        )

    length = dec_input.shape[1]
    enc_rows = [(enc, i * enc_output.shape[1], enc_output.shape[1]) for i in range(rows)]
    column_of = lambda group, i: [g[i] for g in group]
    cb = [cross_back(0)]
    ready = ffn_sums.ready_one(cb[0][3])
    ffn_sums.move_one()
    cb.append(cross_back(1, *ready))
    cb.append(cross_back(2, cb[1][3]))
    ready = ffn_sums.ready_two(cb[2][3])
    ffn_sums.move_two()
    cross_keep, cross_send = weight_grads(
        position,
        [[after(selfs[0][7], *ready)] + column_of(selfs[1:], 7), enc_rows, enc_rows, column_of(crosses, 3)],
        [column_of(cb, 0), column_of(cb, 1), column_of(cb, 2), [(late_gradb, i * length, length) for i in range(rows)]],
    )
    cross_sums = Scatter(position, cross_keep, cross_send)
    ready = ffn_sums.ready_three(cross_keep)
    ffn_sums.move_three()
    sb = [self_back(0, cb[0], *ready)]
    ready = ffn_sums.ready_four(sb[0][3]) + cross_sums.ready_one(sb[0][3])
    ffn_sums.move_four()
    cross_sums.move_one()
    sb.append(self_back(1, cb[1], *ready))
    ffn_total = ffn_sums.total(sb[1][3])
    ffn_sums.move_row()
    ready = cross_sums.ready_two(sb[1][3])
    cross_sums.move_two()
    sb.append(self_back(2, cb[2], ffn_total, *ready))
    ready = cross_sums.ready_three(sb[2][3])
    cross_sums.move_three()
    norms = column_of(selfs, 0)
    self_keep, self_send = weight_grads(
        position,
        [norms, norms, norms, column_of(selfs, 4)],
        [column_of(sb, 0), column_of(sb, 1), column_of(sb, 2), column_of(cb, 4)],
        [column_of(sb, 4), column_of(cb, 5), [after(grad_gain_ffn, *ready)], column_of(sb, 5)],
    )
    self_sums = Scatter(position, self_keep, self_send)
    ready = self_sums.ready_one()
    self_sums.move_one()
    enc_grad = key_value_back(column_of(cb, 1), column_of(cb, 2), after(cross_matrices[1], *ready), cross_matrices[2])
    self_sums.ready_two(enc_grad)
    self_sums.move_two()
    cross_sums.ready_four(self_keep)
    cross_sums.move_four()
    self_sums.ready_three()
    self_sums.move_three()
    cross_sums.total(*self_sums.sent_now())
    cross_sums.move_row()
    self_sums.ready_four()
    self_sums.move_four()
    ffn_sum = ffn_sums.finish(self_keep)
    cross_sum = cross_sums.finish().astype(F32)
    self_sums.total()
    self_sums.move_row()
    self_sum = self_sums.finish().astype(F32)
    inner_rows = features // 8
    pieces = lambda first: jnp.concatenate(
        [
            ffn_sum[p, (4 * b + 2 * first + i) * inner_rows : (4 * b + 2 * first + i + 1) * inner_rows]
            for p in range(PARTS)
            for b in range(blocks)
            for i in range(each // 128)
        ],
        1,
    ).astype(F32)
    start = inner_rows * (4 * each // 128)
    down_sum = jnp.concatenate(
        [
            ffn_sum[:, start + i * down_rows : start + (i + 1) * down_rows]
            for i in range(features // 128)
        ],
        2,
    ).astype(F32)
    small = self_sum[0, inner_rows:]
    small_gains = lax.dynamic_slice(small, (0, shard * gain_rows), (3, gain_rows))
    return (
        out.reshape(dec_input.shape),
        jnp.stack(column_of(sb, 3)),
        enc_grad,
        small_gains[0],
        self_sum[0, :inner_rows],
        self_sum[1, :inner_rows],
        self_sum[2, :inner_rows],
        self_sum[3, :inner_rows],
        small[4 : 4 + table_rows, :HEADS],
        small_gains[1],
        cross_sum[0],
        cross_sum[1],
        cross_sum[2],
        cross_sum[3],
        small_gains[2],
        pieces(0),
        pieces(1),
        down_sum.reshape(wo_ffn.shape),
    )


def solution(mesh):
    placed = (
        P(("rep", "fsdp"), None, None),
        P(("rep", "fsdp"), None, None),
        P(("rep", "fsdp"), None),
        P(("rep", "fsdp"), None),
        P(("rep", "fsdp"), None, None),
        P("fsdp"),
        P("fsdp", None),
        P("fsdp", None),
        P("fsdp", None),
        P("fsdp", None),
        P("fsdp", None),
        P("fsdp"),
        P("fsdp", None),
        P("fsdp", None),
        P("fsdp", None),
        P("fsdp", None),
        P("fsdp"),
        P("fsdp", None),
        P("fsdp", None),
        P("fsdp", None),
    )
    fast = mesh.shape["rep"] == 4 and mesh.shape["fsdp"] == 8
    return jax.shard_map(
        fast_shards if fast else shards,
        mesh=mesh,
        in_specs=placed,
        out_specs=(
            P(("rep", "fsdp"), None, None),
            P(("rep", "fsdp"), None, None),
            P(("rep", "fsdp"), None, None),
            P("fsdp"),
            P("fsdp", None),
            P("fsdp", None),
            P("fsdp", None),
            P("fsdp", None),
            P("fsdp", None),
            P("fsdp"),
            P("fsdp", None),
            P("fsdp", None),
            P("fsdp", None),
            P("fsdp", None),
            P("fsdp"),
            P("fsdp", None),
            P("fsdp", None),
            P("fsdp", None),
        ),
        check_vma=False,
    )
```
